32 devices in a mesh: shots: 2 (over x), slab: 16 (over z, y, core).
Axes of the slice: x: 2, y: 2, z: 4, core: 2. Of those that a mesh axis runs over, the one named last changes fastest.
Arguments:
- fields: float32 [32, 2, 2, 128, 256], P(('shots', 'slab')), parts along dimension 0, may hold values from -6 to 6
- freq_index: int32 [32], P(('shots', 'slab')), parts along dimension 0, may hold values from 0 to 511
- slowness_index: int32 [16, 128, 256], P('slab'), may hold values from 0 to 255
- slowness_table: float32 [256], replicated, may hold values from 1.2 to 2.4
Outputs:
- image: float32 [32, 128, 256], P(('shots', 'slab')), parts along dimension 0
- fields_out: float32 [32, 2, 2, 128, 256], P(('shots', 'slab')), parts along dimension 0
The draws below stay inside these ranges and needn't reach their ends.
There are 2 independent parts, one for each index of `shots`. The reference program is written for one: setup_inputs(seed, part) draws one part's arguments, and reference() takes and returns one part's arrays. A program takes and returns all parts, laid end to end along the dimension named above; an argument that names none is the same for every part. Nothing has to cross between parts.
All inputs are finite; a program needn't handle non-finite values.
Results may differ from the reference program's by a relative error of at most 0.0003.
Values sent between devices are 32-bit elements; how exact they have to be, the bound alone decides.
A program may use at most 64 MiB of HBM per device.

```python
import jax
import jax.numpy as jnp
from jax import lax

NX = 128
NY = 256
STEPS = 1
TICKS = 3
LEVELS = 256
NFREQ = 512
ITEMS = 16
DEPTH = 16


def touch_ends(values, own_key, low, high):
    spot = [jax.random.randint(jax.random.fold_in(own_key, axis), (), 0, length) for axis, length in enumerate(values.shape)]
    widest = values.shape.index(max(values.shape))
    neighbour = spot[:widest] + [(spot[widest] + 1) % values.shape[widest]] + spot[widest + 1:]
    return values.at[tuple(spot)].set(low).at[tuple(neighbour)].set(high)


def levels(own_key, extent, cuts, least, top_value):
    def one(position, shards_of):
        steps = jax.random.uniform(jax.random.fold_in(jax.random.fold_in(own_key, 6), position), (shards_of,), jnp.float32, least / len(cuts), top_value / len(cuts))
        return jnp.repeat(jnp.exp(steps), extent[position] // shards_of).reshape((-1,) + (1,) * (len(extent) - position - 1))

    factor_of = one(*cuts[0])
    for cut in cuts[1:]:
        factor_of = factor_of * one(*cut)
    return factor_of


def noise(key, shape, deviation, most, split=(), kind=jnp.bfloat16):
    level = levels(key, shape, split, -0.22, 0.18) if split else 1.0
    values = jax.random.normal(key, shape, jnp.float32) * deviation * level
    return jnp.minimum(jnp.maximum(values, -most), most).astype(kind)


def setup_inputs(seed: int = 0, part: int = 0) -> dict:
    key_list = jax.random.split(jax.random.key(seed), 5)
    own_keys = jax.random.split(jax.random.fold_in(key_list[4], part), 5)
    fields = noise(own_keys[0], (ITEMS, 2, 2, NX, NY), 1.0, 6.0, ((0, 16),), jnp.float32)
    freq_index = touch_ends(jax.random.randint(own_keys[1], (ITEMS,), 0, NFREQ), jax.random.fold_in(own_keys[1], 1), 0, NFREQ - 1).astype(jnp.int32)
    slowness_index = touch_ends(jax.random.randint(key_list[2], (DEPTH, NX, NY), 0, LEVELS), jax.random.fold_in(key_list[2], 1), 0, LEVELS - 1).astype(jnp.int32)
    slowness_table = jnp.clip(jax.random.uniform(key_list[3], (LEVELS,), jnp.float32, 1.2, 2.4), 1.2, 2.4)
    return {"fields": fields, "freq_index": freq_index, "slowness_index": slowness_index, "slowness_table": slowness_table}


def advance(real_part, imag_part, omega, plane, mean_slow, signs, wave_sq):
    spectrum = jnp.fft.fft2(lax.complex(real_part, imag_part))
    spec_real = jnp.real(spectrum)
    spec_imag = jnp.imag(spectrum)
    k_square = (omega * mean_slow) ** 2
    vertical = jnp.sqrt(jnp.maximum(k_square - wave_sq, 0.0))
    decay = jnp.sqrt(jnp.maximum(wave_sq - k_square, 0.0))
    damping = jnp.exp(-decay)
    cosine = damping * jnp.cos(vertical)
    sine = signs * damping * jnp.sin(vertical)
    shifted_real = spec_real * cosine - spec_imag * sine
    shifted_imag = spec_real * sine + spec_imag * cosine
    back = jnp.fft.ifft2(lax.complex(shifted_real, shifted_imag))
    back_real = jnp.real(back)
    back_imag = jnp.imag(back)
    screen = omega * (plane - mean_slow)
    screen_cos = jnp.cos(screen)
    screen_sin = signs * jnp.sin(screen)
    return (back_real * screen_cos - back_imag * screen_sin, back_real * screen_sin + back_imag * screen_cos)

def reference(fields, freq_index, slowness_index, slowness_table):
    slow = jnp.take(slowness_table, slowness_index, axis=0)
    mean_slow = lax.optimization_barrier(jnp.mean(slow, axis=(1, 2)))
    planes = slow.reshape(ITEMS, STEPS, NX, NY)
    means = mean_slow.reshape(ITEMS, STEPS)
    omega = 1.0 + freq_index.astype(jnp.float32) / NFREQ
    wave_x = jnp.fft.fftfreq(NX).astype(jnp.float32) * (2.0 * jnp.pi)
    wave_y = jnp.fft.fftfreq(NY).astype(jnp.float32) * (2.0 * jnp.pi)
    wave_sq = wave_x[:, None] ** 2 + wave_y[None, :] ** 2
    signs = jnp.array([1.0, -1.0], dtype=jnp.float32).reshape(2, 1, 1)

    def slab_pass(inputs):
        state, frequency, slab_planes, slab_means = inputs
        real_part = state[:, 0]
        imag_part = state[:, 1]
        images = []
        for depth_no in range(STEPS):
            real_part, imag_part = advance(real_part, imag_part, frequency, slab_planes[depth_no], slab_means[depth_no], signs, wave_sq)
            images.append(real_part[0] * real_part[1] + imag_part[0] * imag_part[1])
        return (jnp.stack([real_part, imag_part], axis=1), jnp.stack(images))
    state = fields
    image_raw = jnp.zeros((DEPTH, NX, NY), dtype=jnp.float32)
    for tick_no in range(TICKS):
        if tick_no > 0:
            state = jnp.concatenate([jnp.zeros_like(state[:1]), state[:-1]], axis=0)
            omega = jnp.concatenate([jnp.zeros_like(omega[:1]), omega[:-1]], axis=0)
        state, added = lax.map(slab_pass, (state, omega, planes, means))
        image_raw = image_raw + added.reshape(DEPTH, NX, NY)
    padded = jnp.pad(image_raw, ((1, 1), (0, 0), (0, 0)))
    image = image_raw - 0.25 * (padded[:-2] + padded[2:])
    return (image, state)
```

```python
import functools
import math

import jax
import jax.numpy as jnp
import numpy as np
from jax import lax
from jax.experimental import pallas as pl
from jax.experimental.pallas import tpu as pltpu
from jax.sharding import PartitionSpec as P

NFREQ = 512
CHUNKS = 4

F32 = jnp.float32
BF16 = jnp.bfloat16
PI_HI = 3.140625
PI_LO = math.pi - 3.140625


def dft_table(n):
    turn = np.outer(np.arange(n), np.arange(n)) % n * (2.0 * np.pi / n)
    mats = [np.cos(turn), np.sin(turn), -np.sin(turn)]
    high = [mat.astype(BF16) for mat in mats]
    low = [(mat - h.astype(np.float64)).astype(BF16) for mat, h in zip(mats, high)]
    return np.stack(high + low)


def twiddle_table(ny):
    turn = np.arange(ny // 2) * (2.0 * np.pi / ny)
    rows = np.zeros((8, ny // 2), np.float32)
    rows[0], rows[1] = np.cos(turn), np.sin(turn)
    return rows


def split(value):
    high = value.astype(BF16)
    low = (value - high.astype(F32)).astype(BF16)
    return high, low


def cat(values, axis):
    return jnp.concatenate(values, axis=axis)


def block(a, b, c, d):
    return cat([cat([a, b], 1), cat([c, d], 1)], 0)


def dot_data_left(data, high, low):
    d_high, d_low = split(data)
    return jnp.dot(cat([d_high, d_low, d_high], 1), cat([high, high, low], 0), preferred_element_type=F32)


def dot_data_right(high, low, data):
    d_high, d_low = split(data)
    return jnp.dot(cat([high, high, low], 1), cat([d_high, d_low, d_high], 0), preferred_element_type=F32)


def sincos(x):
    turns = jnp.floor(x * (1.0 / math.pi) + 0.5)
    r = (x - turns * PI_HI) - turns * PI_LO
    sign = 1.0 - 2.0 * (turns - 2.0 * jnp.floor(turns * 0.5))
    r2 = r * r
    sin_p = 1.0 / math.factorial(11) * -1.0
    for k, sg in ((9, 1.0), (7, -1.0), (5, 1.0), (3, -1.0)):
        sin_p = sin_p * r2 + sg / math.factorial(k)
    sin_p = r + r * (r2 * sin_p)
    cos_p = 1.0 / math.factorial(12)
    for k, sg in ((10, -1.0), (8, 1.0), (6, -1.0), (4, 1.0), (2, -1.0), (0, 1.0)):
        cos_p = cos_p * r2 + sg / math.factorial(k)
    return sign * sin_p, sign * cos_p


def kernel(
    count, fields, freq, sidx, table, xs_in, ys_in, tw_in, image_out, fields_out,
    own, mid, made, index, planes, levels, xs, ys, tw, wsq, omegas,
    parts_out, parts_in, tail_out, tail_in, sums_out, sums_in,
    in_sems, far_send, far_recv, tile_send, tile_recv, idx_send, idx_recv,
    part_send, part_recv, sum_send, sum_recv,
):
    me = lax.axis_index("slab")
    nx, ny = index.shape[1:]
    half = ny // 2
    rows = nx // CHUNKS
    odd = lax.rem(me, 2) == 1
    even = jnp.logical_not(odd)
    down = me + 2 < count
    up = me >= 2

    def to(offset):
        return {"slab": jnp.clip(me + offset, 0, count - 1)}

    loads = [
        pltpu.make_async_copy(fields.at[0, 0], own.at[0], in_sems.at[0]),
        pltpu.make_async_copy(xs_in, xs, in_sems.at[1]),
        pltpu.make_async_copy(table, levels, in_sems.at[2]),
        pltpu.make_async_copy(sidx.at[0], index.at[0], in_sems.at[3]),
        pltpu.make_async_copy(ys_in, ys, in_sems.at[4]),
        pltpu.make_async_copy(tw_in, tw, in_sems.at[5]),
        pltpu.make_async_copy(fields.at[0, 1], own.at[1], in_sems.at[6]),
    ]
    for load in loads:
        load.start()

    barrier = pltpu.get_barrier_semaphore()

    @pl.when(odd)
    def _():
        pl.semaphore_signal(barrier, inc=1, device_id=to(-1))

        @pl.when(down)
        def _():
            pl.semaphore_signal(barrier, inc=1, device_id=to(1))

    @pl.when(even)
    def _():
        pl.semaphore_signal(barrier, inc=1, device_id=to(1))

        @pl.when(up)
        def _():
            pl.semaphore_signal(barrier, inc=1, device_id=to(-1))

    @pl.when(down)
    def _():
        pl.semaphore_signal(barrier, inc=1, device_id=to(2))

    @pl.when(up)
    def _():
        pl.semaphore_signal(barrier, inc=1, device_id=to(-2))

    row = lax.broadcasted_iota(jnp.int32, (nx, half), 0)
    wave_x = jnp.where(row < (nx + 1) // 2, row, row - nx).astype(F32) * (2.0 * math.pi / nx)
    lane = lax.broadcasted_iota(jnp.int32, (1, half), 1)
    for parity in (0, 1):
        k = 2 * lane + parity
        wave_y = jnp.where(k < (ny + 1) // 2, k, k - ny).astype(F32) * (2.0 * math.pi / ny)
        wsq[pl.ds(parity * nx, nx)] = wave_x * wave_x + wave_y * wave_y

    omegas[0] = jnp.full((8, 128), 1.0 + freq[0].astype(F32) / NFREQ, F32)

    def look_up(slot):
        pieces = [
            jnp.broadcast_to(levels[pl.ds(j * 128, 128)].reshape(1, 128), (nx, 128))
            for j in range(levels.shape[0] // 128)
        ]
        for h in range(ny // 128):
            cols = pl.ds(h * 128, 128)
            idx = index[slot, :, cols]
            inner = idx & 127
            value = jnp.take_along_axis(pieces[0], inner, axis=1, mode="promise_in_bounds")
            for j in range(1, len(pieces)):
                other = jnp.take_along_axis(pieces[j], inner, axis=1, mode="promise_in_bounds")
                value = jnp.where(idx >= j * 128, other, value)
            planes[slot, :, cols] = value
        columns = jnp.sum(planes[slot], axis=0, keepdims=True)
        return jnp.sum(columns, axis=1, keepdims=True) * (1.0 / (nx * ny))

    def factors(omega, slot, mean_slow):
        q = (omega * mean_slow) ** 2 - wsq[...]
        root = jnp.sqrt(jnp.abs(q))
        sin_v, cos_v = sincos(root)
        moving = q > 0.0
        scale = 1.0 / (nx * ny)
        cos_p = jnp.where(moving, cos_v, jnp.exp(-root)) * scale
        sin_p = jnp.where(moving, sin_v, 0.0) * scale
        return (cos_p, sin_p), sincos(omega * (planes[slot] - mean_slow))

    def step(source, target, which, phase, screen):
        x_c, x_s, x_n = ((xs[i], xs[i + 3]) for i in range(3))
        y_c, y_s, y_n = ((ys[i], ys[i + 3]) for i in range(3))
        x_fwd = [block(x_c[i], x_s[i], x_n[i], x_c[i]) for i in (0, 1)]
        x_inv = [block(x_c[i], x_n[i], x_s[i], x_c[i]) for i in (0, 1)]
        y_fwd = [block(y_c[i], y_n[i], y_s[i], y_c[i]) for i in (0, 1)]
        y_inv = [block(y_c[i], y_s[i], y_n[i], y_c[i]) for i in (0, 1)]
        tw_c, tw_s = tw[:1], tw[1:2]
        cos_p, sin_p = phase
        s_sin, s_cos = screen
        mixed = []
        for f in which:
            spec = dot_data_right(*x_fwd, cat([source[f, 0], source[f, 1]], 0))
            left, right = spec[:, :half], spec[:, half:]
            plus, minus = left + right, left - right
            m_re, m_im = minus[:nx], minus[nx:]
            mixed.append(cat([
                cat([plus[:nx], plus[nx:]], 1),
                cat([m_re * tw_c + m_im * tw_s, m_im * tw_c - m_re * tw_s], 1),
            ], 0))
        spectrum = dot_data_left(cat(mixed, 0), *y_fwd)
        shifted = []
        for at, f in enumerate(which):
            v = spectrum[at * 2 * nx:(at + 1) * 2 * nx]
            v_re, v_im = v[:, :half], v[:, half:]
            if f == 0:
                shifted.append(cat([v_re * cos_p - v_im * sin_p, v_re * sin_p + v_im * cos_p], 1))
            else:
                shifted.append(cat([v_re * cos_p + v_im * sin_p, v_im * cos_p - v_re * sin_p], 1))
        back = dot_data_left(cat(shifted, 0), *y_inv)
        for at, f in enumerate(which):
            b = back[at * 2 * nx:(at + 1) * 2 * nx]
            e_re, e_im = b[:nx, :half], b[:nx, half:]
            t_re, t_im = b[nx:, :half], b[nx:, half:]
            o_re, o_im = t_re * tw_c - t_im * tw_s, t_im * tw_c + t_re * tw_s
            moved = dot_data_right(*x_inv, cat([
                cat([e_re + o_re, e_re - o_re], 1), cat([e_im + o_im, e_im - o_im], 1),
            ], 0))
            b_re, b_im = moved[:nx], moved[nx:]
            if f == 0:
                target[f, 0] = b_re * s_cos - b_im * s_sin
                target[f, 1] = b_re * s_sin + b_im * s_cos
            else:
                target[f, 0] = b_re * s_cos + b_im * s_sin
                target[f, 1] = b_im * s_cos - b_re * s_sin

    def product(ref):
        return ref[0, 0] * ref[1, 0] + ref[0, 1] * ref[1, 1]

    def omega_of(slot):
        return omegas[slot, :1, :1]

    def remote(src, dst, send, recv, offset):
        return pltpu.make_async_remote_copy(
            src_ref=src, dst_ref=dst, send_sem=send, recv_sem=recv, device_id=to(offset)
        )

    def field_copy(f):
        return remote(made.at[f], mid.at[f], far_send.at[f], far_recv.at[f], 2)

    def omega_copy():
        return remote(omegas.at[0], omegas.at[1], far_send.at[2], far_recv.at[2], 2)

    def tile_copy(j):
        part = pl.ds(j * rows, rows)
        return remote(
            made.at[:, :, part], fields_out.at[0, :, :, part], tile_send.at[j], tile_recv.at[j], 2
        )

    def index_copy(offset, slot):
        return remote(sidx.at[0], index.at[slot], idx_send.at[slot], idx_recv.at[slot], offset)

    def part_copy(j):
        return remote(parts_out.at[j], parts_in.at[j], part_send.at[j], part_recv.at[j], 1)

    def tail_copy(j):
        part = pl.ds(j * rows, rows)
        return remote(
            tail_out.at[part], tail_in.at[part], part_send.at[3 + j], part_recv.at[3 + j], 1
        )

    def sum_copy(which, slot, offset):
        return remote(sums_out.at[which], sums_in.at[slot], sum_send.at[slot], sum_recv.at[slot], offset)

    @pl.when(odd)
    def _():
        loads[2].wait()
        loads[3].wait()
        mean_own = look_up(0)
        phase, screen = factors(omega_of(0), 0, mean_own)
        for n in (0, 1, 4, 5):
            loads[n].wait()
        step(own, made, (0,), phase, screen)
        pl.semaphore_wait(barrier, 1 + jnp.where(down, 2, 0) + jnp.where(up, 1, 0))

        @pl.when(down)
        def _():
            omega_copy().start()
            field_copy(0).start()

        index_copy(-1, 1).start()
        loads[6].wait()
        step(own, made, (1,), phase, screen)

        @pl.when(down)
        def _():
            field_copy(1).start()

        @pl.when(jnp.logical_not(up))
        def _():
            mid[...] = jnp.zeros(mid.shape, F32)
            omegas[1] = jnp.zeros((8, 128), F32)

        @pl.when(jnp.logical_not(down))
        def _():
            parts_in[2] = jnp.zeros((nx, ny), F32)
            sums_in[2] = jnp.zeros((nx, ny), F32)

        raw = product(made)
        index_copy(1, 1).wait_recv()

        @pl.when(up)
        def _():
            omega_copy().wait_recv()

        mean_low = look_up(1)
        phase_0, screen_0 = factors(omega_of(1), 1, mean_low)
        phase_1, screen_1 = factors(omega_of(1), 0, mean_own)

        @pl.when(up)
        def _():
            field_copy(0).wait_recv()

        step(mid, own, (0,), phase_0, screen_0)
        step(own, fields_out.at[0], (0,), phase_1, screen_1)

        @pl.when(up)
        def _():
            field_copy(1).wait_recv()

        step(mid, own, (1,), phase_0, screen_0)
        part_copy(0).wait_recv()
        sums_out[0] = parts_in[0] + product(own)
        sum_copy(0, 0, -1).start()

        @pl.when(up)
        def _():
            sum_copy(0, 2, -2).start()

        step(own, fields_out.at[0], (1,), phase_1, screen_1)
        part_copy(1).wait_recv()
        sums_out[1] = raw + parts_in[1] + product(fields_out.at[0])
        sum_copy(1, 1, -1).start()

        @pl.when(down)
        def _():
            sum_copy(1, 3, 1).start()
            part_copy(2).wait_recv()
            sum_copy(0, 2, -2).wait_recv()

        image_out[0] = sums_out[1] - 0.25 * (sums_out[0] + parts_in[2] + sums_in[2])

        @pl.when(up)
        def _():
            for j in range(CHUNKS):
                tail_copy(j).wait_recv()
            image_out[0] = image_out[0] - 0.25 * tail_in[...]

        index_copy(-1, 1).wait_send()
        sum_copy(0, 0, -1).wait_send()
        sum_copy(1, 1, -1).wait_send()

        @pl.when(down)
        def _():
            omega_copy().wait_send()
            field_copy(0).wait_send()
            field_copy(1).wait_send()
            sum_copy(1, 3, 1).wait_send()

        @pl.when(up)
        def _():
            sum_copy(0, 2, -2).wait_send()

    @pl.when(even)
    def _():
        pl.semaphore_wait(barrier, 1 + jnp.where(down, 1, 0) + jnp.where(up, 2, 0))

        @pl.when(up)
        def _():
            index_copy(-2, 2).start()

        index_copy(1, 1).start()

        @pl.when(jnp.logical_not(up))
        def _():
            fields_out[0] = jnp.zeros(fields_out.shape[1:], F32)
            sums_in[3] = jnp.zeros((nx, ny), F32)

        loads[2].wait()
        loads[3].wait()
        mean_slow = look_up(0)
        phase, screen = factors(omega_of(0), 0, mean_slow)
        for n in (0, 1, 4, 5, 6):
            loads[n].wait()
        step(own, mid, (0, 1), phase, screen)
        parts_out[0] = product(mid)
        part_copy(0).start()

        index_copy(-1, 1).wait_recv()
        mean_slow = look_up(1)
        phase, screen = factors(omega_of(0), 1, mean_slow)
        step(mid, own, (0, 1), phase, screen)
        parts_out[1] = product(own)
        part_copy(1).start()

        @pl.when(down)
        def _():
            index_copy(-2, 2).wait_recv()
            mean_slow = look_up(2)
            phase, screen = factors(omega_of(0), 2, mean_slow)
            step(own, made, (0, 1), phase, screen)
            for j in range(CHUNKS):
                tile_copy(j).start()
            parts_out[2] = product(made)
            part_copy(2).start()

        sum_copy(0, 0, -1).wait_recv()
        sum_copy(1, 1, -1).wait_recv()
        image_out[0] = sums_in[0] - 0.25 * sums_in[1]

        @pl.when(up)
        def _():
            for j in range(CHUNKS):
                part = pl.ds(j * rows, rows)
                tile_copy(j).wait_recv()
                tail_out[part] = product(fields_out.at[0, :, :, part])
                tail_copy(j).start()
            sum_copy(1, 3, 1).wait_recv()
            image_out[0] = image_out[0] + tail_out[...] - 0.25 * sums_in[3]
            for j in range(CHUNKS):
                tail_copy(j).wait_send()
            index_copy(-2, 2).wait_send()

        index_copy(1, 1).wait_send()
        part_copy(0).wait_send()
        part_copy(1).wait_send()

        @pl.when(down)
        def _():
            for j in range(CHUNKS):
                tile_copy(j).wait_send()
            part_copy(2).wait_send()


def store(image, fields, image_out, fields_out, sems):
    copies = [
        pltpu.make_async_copy(fields, fields_out, sems.at[0]),
        pltpu.make_async_copy(image, image_out, sems.at[1]),
    ]
    for copy in copies:
        copy.start()
    for copy in copies:
        copy.wait()


def body(fields, freq_index, slowness_index, slowness_table):
    nx, ny = slowness_index.shape[1:]
    count = lax.axis_size("slab")
    assert slowness_index.shape[0] == 1 and count % 2 == 0
    half = ny // 2
    xs, ys, tw = dft_table(nx), dft_table(half), twiddle_table(ny)
    any_spec = pl.BlockSpec(memory_space=pl.ANY)
    vmem_spec = pl.BlockSpec(memory_space=pltpu.VMEM)
    plane = (nx, ny)
    dma = pltpu.SemaphoreType.DMA
    image, moved = pl.pallas_call(
        functools.partial(kernel, count),
        out_shape=(pltpu.VMEM((1, nx, ny), F32), pltpu.VMEM(fields.shape, F32)),
        in_specs=[
            any_spec, pl.BlockSpec(memory_space=pltpu.SMEM), any_spec, any_spec,
            any_spec, any_spec, any_spec,
        ],
        out_specs=(vmem_spec, vmem_spec),
        scratch_shapes=[
            pltpu.VMEM((2, 2) + plane, F32),
            pltpu.VMEM((2, 2) + plane, F32),
            pltpu.VMEM((2, 2) + plane, F32),
            pltpu.VMEM((3,) + plane, jnp.int32),
            pltpu.VMEM((3,) + plane, F32),
            pltpu.VMEM(slowness_table.shape, F32),
            pltpu.VMEM(xs.shape, BF16),
            pltpu.VMEM(ys.shape, BF16),
            pltpu.VMEM(tw.shape, F32),
            pltpu.VMEM((2 * nx, half), F32),
            pltpu.VMEM((2, 8, 128), F32),
            pltpu.VMEM((3,) + plane, F32),
            pltpu.VMEM((3,) + plane, F32),
            pltpu.VMEM(plane, F32),
            pltpu.VMEM(plane, F32),
            pltpu.VMEM((2,) + plane, F32),
            pltpu.VMEM((4,) + plane, F32),
            dma((7,)),
            dma((3,)),
            dma((3,)),
            dma((CHUNKS,)),
            dma((CHUNKS,)),
            dma((3,)),
            dma((3,)),
            dma((3 + CHUNKS,)),
            dma((3 + CHUNKS,)),
            dma((4,)),
            dma((4,)),
        ],
        compiler_params=pltpu.CompilerParams(collective_id=0, has_side_effects=True),
        name="slabs",
    )(
        fields, freq_index, slowness_index, slowness_table,
        jnp.asarray(xs), jnp.asarray(ys), jnp.asarray(tw),
    )
    return pl.pallas_call(
        store,
        out_shape=(
            jax.ShapeDtypeStruct((1, nx, ny), F32),
            jax.ShapeDtypeStruct(fields.shape, F32),
        ),
        in_specs=[vmem_spec, vmem_spec],
        out_specs=(any_spec, any_spec),
        scratch_shapes=[dma((2,))],
        name="store",
    )(
        pltpu.with_memory_space_constraint(image, pltpu.VMEM),
        pltpu.with_memory_space_constraint(moved, pltpu.VMEM),
    )


def solution(mesh):
    return jax.shard_map(
        body,
        mesh=mesh,
        in_specs=(
            P(("shots", "slab"), None, None, None, None),
            P(("shots", "slab")),
            P("slab", None, None),
            P(),
        ),
        out_specs=(P(("shots", "slab"), None, None), P(("shots", "slab"), None, None, None, None)),
        check_vma=False,
    )
```

```python
import functools
import math

import jax
import jax.numpy as jnp
import numpy as np
from jax import lax
from jax.experimental import pallas as pl
from jax.experimental.pallas import tpu as pltpu
from jax.sharding import PartitionSpec as P

NFREQ = 512
CHUNKS = 4

F32 = jnp.float32
BF16 = jnp.bfloat16
PI_HI = 3.140625
PI_LO = math.pi - 3.140625


def dft_table(n):
    turn = np.outer(np.arange(n), np.arange(n)) % n * (2.0 * np.pi / n)
    mats = [np.cos(turn), np.sin(turn), -np.sin(turn)]
    high = [mat.astype(BF16) for mat in mats]
    low = [(mat - h.astype(np.float64)).astype(BF16) for mat, h in zip(mats, high)]
    return np.stack(high + low)


def twiddle_table(ny):
    turn = np.arange(ny // 2) * (2.0 * np.pi / ny)
    rows = np.zeros((8, ny // 2), np.float32)
    rows[0], rows[1] = np.cos(turn), np.sin(turn)
    return rows


def split(value):
    high = value.astype(BF16)
    low = (value - high.astype(F32)).astype(BF16)
    return high, low


def cat(values, axis):
    return jnp.concatenate(values, axis=axis)


def block(a, b, c, d):
    return cat([cat([a, b], 1), cat([c, d], 1)], 0)


def dot_data_left(data, high, low):
    d_high, d_low = split(data)
    return jnp.dot(cat([d_high, d_low, d_high], 1), cat([high, high, low], 0), preferred_element_type=F32)


def dot_data_right(high, low, data):
    d_high, d_low = split(data)
    return jnp.dot(cat([high, high, low], 1), cat([d_high, d_low, d_high], 0), preferred_element_type=F32)


def sincos(x):
    turns = jnp.floor(x * (1.0 / math.pi) + 0.5)
    r = (x - turns * PI_HI) - turns * PI_LO
    sign = 1.0 - 2.0 * (turns - 2.0 * jnp.floor(turns * 0.5))
    r2 = r * r
    sin_p = 1.0 / math.factorial(11) * -1.0
    for k, sg in ((9, 1.0), (7, -1.0), (5, 1.0), (3, -1.0)):
        sin_p = sin_p * r2 + sg / math.factorial(k)
    sin_p = r + r * (r2 * sin_p)
    cos_p = 1.0 / math.factorial(12)
    for k, sg in ((10, -1.0), (8, 1.0), (6, -1.0), (4, 1.0), (2, -1.0), (0, 1.0)):
        cos_p = cos_p * r2 + sg / math.factorial(k)
    return sign * sin_p, sign * cos_p


def kernel(
    count, fields, freq, sidx, table, xs_in, ys_in, tw_in, image_out, fields_out,
    own, work, made, got, index, planes, levels, xs, ys, tw, wsq, omegas, means, turns,
    part_out, part_in, raw_out, raw_near, raw_far, first,
    in_sems, far_send, far_recv, tile_send, tile_recv, pair_send, pair_recv,
    near_send, near_recv, edge_send, edge_recv,
):
    me = lax.axis_index("slab")
    nx, ny = index.shape[1:]
    half = ny // 2
    rows = nx // CHUNKS
    odd = lax.rem(me, 2) == 1
    even = jnp.logical_not(odd)
    down = me + 2 < count
    up = me >= 2

    def to(offset):
        return {"slab": jnp.clip(me + offset, 0, count - 1)}

    loads = [
        pltpu.make_async_copy(fields.at[0, 0], own.at[0], in_sems.at[0]),
        pltpu.make_async_copy(xs_in, xs, in_sems.at[1]),
        pltpu.make_async_copy(table, levels, in_sems.at[2]),
        pltpu.make_async_copy(sidx.at[0], index.at[0], in_sems.at[3]),
        pltpu.make_async_copy(ys_in, ys, in_sems.at[4]),
        pltpu.make_async_copy(tw_in, tw, in_sems.at[5]),
        pltpu.make_async_copy(fields.at[0, 1], own.at[1], in_sems.at[6]),
    ]
    for load in loads:
        load.start()

    barrier = pltpu.get_barrier_semaphore()

    @pl.when(odd)
    def _():
        pl.semaphore_signal(barrier, inc=1, device_id=to(-1))

        @pl.when(down)
        def _():
            pl.semaphore_signal(barrier, inc=1, device_id=to(1))

    @pl.when(even)
    def _():
        pl.semaphore_signal(barrier, inc=1, device_id=to(1))

        @pl.when(up)
        def _():
            pl.semaphore_signal(barrier, inc=1, device_id=to(-1))

    @pl.when(down)
    def _():
        pl.semaphore_signal(barrier, inc=1, device_id=to(2))

    @pl.when(up)
    def _():
        pl.semaphore_signal(barrier, inc=1, device_id=to(-2))

    row = lax.broadcasted_iota(jnp.int32, (nx, half), 0)
    wave_x = jnp.where(row < (nx + 1) // 2, row, row - nx).astype(F32) * (2.0 * math.pi / nx)
    lane = lax.broadcasted_iota(jnp.int32, (1, half), 1)
    for parity in (0, 1):
        k = 2 * lane + parity
        wave_y = jnp.where(k < (ny + 1) // 2, k, k - ny).astype(F32) * (2.0 * math.pi / ny)
        wsq[pl.ds(parity * nx, nx)] = wave_x * wave_x + wave_y * wave_y

    omegas[0] = jnp.full((8, 128), 1.0 + freq[0].astype(F32) / NFREQ, F32)

    @pl.when(jnp.logical_not(up))
    def _():
        got[...] = jnp.zeros(got.shape, F32)
        omegas[1] = jnp.zeros((8, 128), F32)

    @pl.when(jnp.logical_not(jnp.logical_or(odd & down, even & up)))
    def _():
        raw_far[...] = jnp.zeros((nx, ny), F32)

    def look_up(slot):
        pieces = [
            jnp.broadcast_to(levels[pl.ds(j * 128, 128)].reshape(1, 128), (nx, 128))
            for j in range(levels.shape[0] // 128)
        ]
        for h in range(ny // 128):
            cols = pl.ds(h * 128, 128)
            idx = index[slot, :, cols]
            inner = idx & 127
            value = jnp.take_along_axis(pieces[0], inner, axis=1, mode="promise_in_bounds")
            for j in range(1, len(pieces)):
                other = jnp.take_along_axis(pieces[j], inner, axis=1, mode="promise_in_bounds")
                value = jnp.where(idx >= j * 128, other, value)
            planes[slot, :, cols] = value
        columns = jnp.sum(planes[slot], axis=0, keepdims=True)
        return jnp.sum(columns, axis=1, keepdims=True) * (1.0 / (nx * ny))

    def phases(omega, mean_slow):
        q = (omega * mean_slow) ** 2 - wsq[...]
        root = jnp.sqrt(jnp.abs(q))
        sin_v, cos_v = sincos(root)
        moving = q > 0.0
        scale = 1.0 / (nx * ny)
        cos_p = jnp.where(moving, cos_v, jnp.exp(-root)) * scale
        sin_p = jnp.where(moving, sin_v, 0.0) * scale
        return cos_p, sin_p

    def screens(omega, slot, mean_slow):
        return sincos(omega * (planes[slot] - mean_slow))

    def spectral(source, which, phase):
        x_c, x_s, x_n = ((xs[i], xs[i + 3]) for i in range(3))
        y_c, y_s, y_n = ((ys[i], ys[i + 3]) for i in range(3))
        x_fwd = [block(x_c[i], x_s[i], x_n[i], x_c[i]) for i in (0, 1)]
        x_inv = [block(x_c[i], x_n[i], x_s[i], x_c[i]) for i in (0, 1)]
        y_fwd = [block(y_c[i], y_n[i], y_s[i], y_c[i]) for i in (0, 1)]
        y_inv = [block(y_c[i], y_s[i], y_n[i], y_c[i]) for i in (0, 1)]
        tw_c, tw_s = tw[:1], tw[1:2]
        cos_p, sin_p = phase
        mixed = []
        for f in which:
            spec = dot_data_right(*x_fwd, cat([source[f, 0], source[f, 1]], 0))
            left, right = spec[:, :half], spec[:, half:]
            plus, minus = left + right, left - right
            m_re, m_im = minus[:nx], minus[nx:]
            mixed.append(cat([
                cat([plus[:nx], plus[nx:]], 1),
                cat([m_re * tw_c + m_im * tw_s, m_im * tw_c - m_re * tw_s], 1),
            ], 0))
        spectrum = dot_data_left(cat(mixed, 0), *y_fwd)
        shifted = []
        for at, f in enumerate(which):
            v = spectrum[at * 2 * nx:(at + 1) * 2 * nx]
            v_re, v_im = v[:, :half], v[:, half:]
            if f == 0:
                shifted.append(cat([v_re * cos_p - v_im * sin_p, v_re * sin_p + v_im * cos_p], 1))
            else:
                shifted.append(cat([v_re * cos_p + v_im * sin_p, v_im * cos_p - v_re * sin_p], 1))
        back = dot_data_left(cat(shifted, 0), *y_inv)
        out = []
        for at, f in enumerate(which):
            b = back[at * 2 * nx:(at + 1) * 2 * nx]
            e_re, e_im = b[:nx, :half], b[:nx, half:]
            t_re, t_im = b[nx:, :half], b[nx:, half:]
            o_re, o_im = t_re * tw_c - t_im * tw_s, t_im * tw_c + t_re * tw_s
            moved = dot_data_right(*x_inv, cat([
                cat([e_re + o_re, e_re - o_re], 1), cat([e_im + o_im, e_im - o_im], 1),
            ], 0))
            out.append((moved[:nx], moved[nx:]))
        return out

    def turned(f, b_re, b_im, screen):
        s_sin, s_cos = screen
        if f == 0:
            return b_re * s_cos - b_im * s_sin, b_re * s_sin + b_im * s_cos
        return b_re * s_cos + b_im * s_sin, b_im * s_cos - b_re * s_sin

    def step(source, target, which, phase, screen):
        for f, (b_re, b_im) in zip(which, spectral(source, which, phase)):
            target[f, 0], target[f, 1] = turned(f, b_re, b_im, screen)

    def product(ref):
        return ref[0, 0] * ref[1, 0] + ref[0, 1] * ref[1, 1]

    def omega_of(slot):
        return omegas[slot, :1, :1]

    def remote(src, dst, send, recv, offset):
        return pltpu.make_async_remote_copy(
            src_ref=src, dst_ref=dst, send_sem=send, recv_sem=recv, device_id=to(offset)
        )

    def field_copy(f):
        return remote(made.at[f], got.at[f], far_send.at[f], far_recv.at[f], 2)

    def omega_copy():
        return remote(omegas.at[0], omegas.at[1], far_send.at[2], far_recv.at[2], 2)

    def mean_copy():
        return remote(means.at[0], means.at[1], far_send.at[3], far_recv.at[3], -2)

    def tile_copy(j):
        part = pl.ds(j * rows, rows)
        return remote(
            made.at[:, :, part], got.at[:, :, part], tile_send.at[j], tile_recv.at[j], 2
        )

    def index_copy(offset):
        return remote(sidx.at[0], index.at[1], pair_send.at[0], pair_recv.at[0], offset)

    def part_copy(offset):
        return remote(part_out, part_in, pair_send.at[1], pair_recv.at[1], offset)

    def near_copy(j, offset):
        part = pl.ds(j * rows, rows)
        return remote(raw_out.at[part], raw_near.at[part], near_send.at[j], near_recv.at[j], offset)

    def edge_copy(j, offset):
        part = pl.ds(j * rows, rows)
        return remote(raw_out.at[part], raw_far.at[part], edge_send.at[j], edge_recv.at[j], offset)

    chunks = range(CHUNKS)

    @pl.when(odd)
    def _():
        for load in loads[:6]:
            load.wait()
        mean_own = look_up(0)
        phase = phases(omega_of(0), mean_own)
        screen_own = screens(omega_of(0), 0, mean_own)
        step(own, made, (0,), phase, screen_own)
        pl.semaphore_wait(barrier, 1 + jnp.where(down, 2, 0) + jnp.where(up, 1, 0))

        @pl.when(down)
        def _():
            omega_copy().start()
            field_copy(0).start()

        index_copy(-1).start()
        loads[6].wait()
        step(own, made, (1,), phase, screen_own)

        @pl.when(down)
        def _():
            field_copy(1).start()

        first[...] = product(made)
        index_copy(1).wait_recv()

        @pl.when(up)
        def _():
            omega_copy().wait_recv()

        mean_low = look_up(1)
        phase_0 = phases(omega_of(1), mean_low)
        screen_0 = screens(omega_of(1), 1, mean_low)
        phase_1 = phases(omega_of(1), mean_own)
        screen_1 = screens(omega_of(1), 0, mean_own)

        @pl.when(up)
        def _():
            field_copy(0).wait_recv()

        step(got, work, (0,), phase_0, screen_0)
        step(work, fields_out.at[0], (0,), phase_1, screen_1)

        @pl.when(up)
        def _():
            field_copy(1).wait_recv()

        step(got, work, (1,), phase_0, screen_0)
        part_out[...] = product(work)
        part_copy(-1).start()
        step(work, fields_out.at[0], (1,), phase_1, screen_1)
        part_copy(1).wait_recv()
        raw_out[...] = first[...] + part_in[...] + product(fields_out.at[0])
        for j in chunks:
            near_copy(j, -1).start()

        @pl.when(down)
        def _():
            for j in chunks:
                edge_copy(j, 1).start()

        for j in chunks:
            part = pl.ds(j * rows, rows)
            near_copy(j, 1).wait_recv()

            @pl.when(down)
            def _():
                edge_copy(j, -1).wait_recv()

            image_out[0, part] = raw_out[part] - 0.25 * (raw_near[part] + raw_far[part])

        index_copy(-1).wait_send()
        part_copy(-1).wait_send()
        for j in chunks:
            near_copy(j, -1).wait_send()

        @pl.when(down)
        def _():
            omega_copy().wait_send()
            field_copy(0).wait_send()
            field_copy(1).wait_send()
            for j in chunks:
                edge_copy(j, 1).wait_send()

    @pl.when(even)
    def _():
        for load in loads[:6]:
            load.wait()
        mean_own = look_up(0)
        means[0] = jnp.broadcast_to(mean_own, (8, 128))
        pl.semaphore_wait(barrier, 1 + jnp.where(down, 1, 0) + jnp.where(up, 2, 0))

        @pl.when(up)
        def _():
            mean_copy().start()

        @pl.when(down)
        def _():
            omega_copy().start()

        index_copy(1).start()
        loads[6].wait()
        phase = phases(omega_of(0), mean_own)
        screen = screens(omega_of(0), 0, mean_own)
        step(own, work, (0, 1), phase, screen)
        first[...] = product(work)

        index_copy(-1).wait_recv()
        mean_next = look_up(1)
        phase = phases(omega_of(0), mean_next)
        screen = screens(omega_of(0), 1, mean_next)
        step(work, own, (0, 1), phase, screen)
        part_out[...] = product(own)
        part_copy(1).start()

        @pl.when(down)
        def _():
            mean_copy().wait_recv()
            phase = phases(omega_of(0), means[1, :1, :1])
            for f, (b_re, b_im) in zip((0, 1), spectral(own, (0, 1), phase)):
                made[f, 0], made[f, 1] = b_re, b_im
            for j in chunks:
                tile_copy(j).start()

        @pl.when(up)
        def _():
            omega_copy().wait_recv()

        turns[0], turns[1] = screens(omega_of(1), 0, means[0, :1, :1])
        part_copy(-1).wait_recv()
        first[...] = first[...] + part_in[...]

        for j in chunks:
            part = pl.ds(j * rows, rows)

            @pl.when(up)
            def _():
                tile_copy(j).wait_recv()

            screen = turns[0, part], turns[1, part]
            s_re, s_im = turned(0, got[0, 0, part], got[0, 1, part], screen)
            r_re, r_im = turned(1, got[1, 0, part], got[1, 1, part], screen)
            raw_out[part] = first[part] + s_re * r_re + s_im * r_im
            fields_out[0, 0, 0, part], fields_out[0, 0, 1, part] = s_re, s_im
            fields_out[0, 1, 0, part], fields_out[0, 1, 1, part] = r_re, r_im
            near_copy(j, 1).start()

            @pl.when(up)
            def _():
                edge_copy(j, -1).start()

        for j in chunks:
            part = pl.ds(j * rows, rows)
            near_copy(j, -1).wait_recv()

            @pl.when(up)
            def _():
                edge_copy(j, 1).wait_recv()

            image_out[0, part] = raw_out[part] - 0.25 * (raw_near[part] + raw_far[part])

        index_copy(1).wait_send()
        part_copy(1).wait_send()
        for j in chunks:
            near_copy(j, 1).wait_send()

        @pl.when(down)
        def _():
            omega_copy().wait_send()
            for j in chunks:
                tile_copy(j).wait_send()

        @pl.when(up)
        def _():
            mean_copy().wait_send()
            for j in chunks:
                edge_copy(j, -1).wait_send()


def store(image, fields, image_out, fields_out, sems):
    copies = [
        pltpu.make_async_copy(fields, fields_out, sems.at[0]),
        pltpu.make_async_copy(image, image_out, sems.at[1]),
    ]
    for copy in copies:
        copy.start()
    for copy in copies:
        copy.wait()


def body(fields, freq_index, slowness_index, slowness_table):
    nx, ny = slowness_index.shape[1:]
    count = lax.axis_size("slab")
    assert slowness_index.shape[0] == 1 and count % 2 == 0
    half = ny // 2
    xs, ys, tw = dft_table(nx), dft_table(half), twiddle_table(ny)
    any_spec = pl.BlockSpec(memory_space=pl.ANY)
    vmem_spec = pl.BlockSpec(memory_space=pltpu.VMEM)
    plane = (nx, ny)
    dma = pltpu.SemaphoreType.DMA
    image, moved = pl.pallas_call(
        functools.partial(kernel, count),
        out_shape=(pltpu.VMEM((1, nx, ny), F32), pltpu.VMEM(fields.shape, F32)),
        in_specs=[
            any_spec, pl.BlockSpec(memory_space=pltpu.SMEM), any_spec, any_spec,
            any_spec, any_spec, any_spec,
        ],
        out_specs=(vmem_spec, vmem_spec),
        scratch_shapes=[
            pltpu.VMEM((2, 2) + plane, F32),
            pltpu.VMEM((2, 2) + plane, F32),
            pltpu.VMEM((2, 2) + plane, F32),
            pltpu.VMEM((2, 2) + plane, F32),
            pltpu.VMEM((2,) + plane, jnp.int32),
            pltpu.VMEM((2,) + plane, F32),
            pltpu.VMEM(slowness_table.shape, F32),
            pltpu.VMEM(xs.shape, BF16),
            pltpu.VMEM(ys.shape, BF16),
            pltpu.VMEM(tw.shape, F32),
            pltpu.VMEM((2 * nx, half), F32),
            pltpu.VMEM((2, 8, 128), F32),
            pltpu.VMEM((2, 8, 128), F32),
            pltpu.VMEM((2,) + plane, F32),
            pltpu.VMEM(plane, F32),
            pltpu.VMEM(plane, F32),
            pltpu.VMEM(plane, F32),
            pltpu.VMEM(plane, F32),
            pltpu.VMEM(plane, F32),
            pltpu.VMEM(plane, F32),
            dma((7,)),
            dma((4,)),
            dma((4,)),
            dma((CHUNKS,)),
            dma((CHUNKS,)),
            dma((2,)),
            dma((2,)),
            dma((CHUNKS,)),
            dma((CHUNKS,)),
            dma((CHUNKS,)),
            dma((CHUNKS,)),
        ],
        compiler_params=pltpu.CompilerParams(collective_id=0, has_side_effects=True),
        name="slabs",
    )(
        fields, freq_index, slowness_index, slowness_table,
        jnp.asarray(xs), jnp.asarray(ys), jnp.asarray(tw),
    )
    return pl.pallas_call(
        store,
        out_shape=(
            jax.ShapeDtypeStruct((1, nx, ny), F32),
            jax.ShapeDtypeStruct(fields.shape, F32),
        ),
        in_specs=[vmem_spec, vmem_spec],
        out_specs=(any_spec, any_spec),
        scratch_shapes=[dma((2,))],
        name="store",
    )(
        pltpu.with_memory_space_constraint(image, pltpu.VMEM),
        pltpu.with_memory_space_constraint(moved, pltpu.VMEM),
    )


def solution(mesh):
    return jax.shard_map(
        body,
        mesh=mesh,
        in_specs=(
            P(("shots", "slab"), None, None, None, None),
            P(("shots", "slab")),
            P("slab", None, None),
            P(),
        ),
        out_specs=(P(("shots", "slab"), None, None), P(("shots", "slab"), None, None, None, None)),
        check_vma=False,
    )
```

```python
import functools
import math

import jax
import jax.numpy as jnp
import numpy as np
from jax import lax
from jax.experimental import pallas as pl
from jax.experimental.pallas import tpu as pltpu
from jax.sharding import PartitionSpec as P

NFREQ = 512
SHARES = (3, 2, 2, 1)
CHUNKS = len(SHARES)

F32 = jnp.float32
BF16 = jnp.bfloat16
PI_HI = 3.140625
PI_LO = math.pi - 3.140625


def dft_table(n):
    turn = np.outer(np.arange(n), np.arange(n)) % n * (2.0 * np.pi / n)
    mats = [np.cos(turn), np.sin(turn), -np.sin(turn)]
    high = [mat.astype(BF16) for mat in mats]
    low = [(mat - h.astype(np.float64)).astype(BF16) for mat, h in zip(mats, high)]
    return np.stack(high + low)


def twiddle_table(ny):
    turn = np.arange(ny // 2) * (2.0 * np.pi / ny)
    rows = np.zeros((8, ny // 2), np.float32)
    rows[0], rows[1] = np.cos(turn), np.sin(turn)
    return rows


def split(value):
    high = value.astype(BF16)
    low = (value - high.astype(F32)).astype(BF16)
    return high, low


def cat(values, axis):
    return jnp.concatenate(values, axis=axis)


def block(a, b, c, d):
    return cat([cat([a, b], 1), cat([c, d], 1)], 0)


def dot_data_left(data, high, low):
    d_high, d_low = split(data)
    return jnp.dot(cat([d_high, d_low, d_high], 1), cat([high, high, low], 0), preferred_element_type=F32)


def dot_data_right(high, low, data):
    d_high, d_low = split(data)
    return jnp.dot(cat([high, high, low], 1), cat([d_high, d_low, d_high], 0), preferred_element_type=F32)


def sincos(x):
    turns = jnp.floor(x * (1.0 / math.pi) + 0.5)
    r = (x - turns * PI_HI) - turns * PI_LO
    sign = 1.0 - 2.0 * (turns - 2.0 * jnp.floor(turns * 0.5))
    r2 = r * r
    sin_p = 1.0 / math.factorial(11) * -1.0
    for k, sg in ((9, 1.0), (7, -1.0), (5, 1.0), (3, -1.0)):
        sin_p = sin_p * r2 + sg / math.factorial(k)
    sin_p = r + r * (r2 * sin_p)
    cos_p = 1.0 / math.factorial(12)
    for k, sg in ((10, -1.0), (8, 1.0), (6, -1.0), (4, 1.0), (2, -1.0), (0, 1.0)):
        cos_p = cos_p * r2 + sg / math.factorial(k)
    return sign * sin_p, sign * cos_p


def kernel(
    count, fields, freq, sidx, table, xs_in, ys_in, tw_in, image_out, fields_out,
    own, work, made, got, index, planes, levels, xs, ys, tw, wsq, omegas, means, turns,
    part_out, part_in, raw_out, raw_near, raw_far, first,
    in_sems, far_send, far_recv, tile_send, tile_recv, pair_send, pair_recv,
    near_send, near_recv, edge_send, edge_recv,
):
    me = lax.axis_index("slab")
    nx, ny = index.shape[1:]
    half = ny // 2
    unit = nx // sum(SHARES)
    starts = [unit * sum(SHARES[:j]) for j in range(CHUNKS)]

    def part_of(j):
        return pl.ds(starts[j], unit * SHARES[j])

    odd = lax.rem(me, 2) == 1
    even = jnp.logical_not(odd)
    down = me + 2 < count
    up = me >= 2

    def to(offset):
        return {"slab": jnp.clip(me + offset, 0, count - 1)}

    loads = [
        pltpu.make_async_copy(fields.at[0, 0], own.at[0], in_sems.at[0]),
        pltpu.make_async_copy(xs_in, xs, in_sems.at[1]),
        pltpu.make_async_copy(table, levels, in_sems.at[2]),
        pltpu.make_async_copy(sidx.at[0], index.at[0], in_sems.at[3]),
        pltpu.make_async_copy(ys_in, ys, in_sems.at[4]),
        pltpu.make_async_copy(tw_in, tw, in_sems.at[5]),
        pltpu.make_async_copy(fields.at[0, 1], own.at[1], in_sems.at[6]),
    ]
    for load in loads:
        load.start()

    barrier = pltpu.get_barrier_semaphore()

    @pl.when(odd)
    def _():
        pl.semaphore_signal(barrier, inc=1, device_id=to(-1))

        @pl.when(down)
        def _():
            pl.semaphore_signal(barrier, inc=1, device_id=to(1))

    @pl.when(even)
    def _():
        pl.semaphore_signal(barrier, inc=1, device_id=to(1))

        @pl.when(up)
        def _():
            pl.semaphore_signal(barrier, inc=1, device_id=to(-1))

    @pl.when(down)
    def _():
        pl.semaphore_signal(barrier, inc=1, device_id=to(2))

    @pl.when(up)
    def _():
        pl.semaphore_signal(barrier, inc=1, device_id=to(-2))

    row = lax.broadcasted_iota(jnp.int32, (nx, half), 0)
    wave_x = jnp.where(row < (nx + 1) // 2, row, row - nx).astype(F32) * (2.0 * math.pi / nx)
    lane = lax.broadcasted_iota(jnp.int32, (1, half), 1)
    for parity in (0, 1):
        k = 2 * lane + parity
        wave_y = jnp.where(k < (ny + 1) // 2, k, k - ny).astype(F32) * (2.0 * math.pi / ny)
        wsq[pl.ds(parity * nx, nx)] = wave_x * wave_x + wave_y * wave_y

    omegas[0] = jnp.full((8, 128), 1.0 + freq[0].astype(F32) / NFREQ, F32)

    @pl.when(jnp.logical_not(up))
    def _():
        got[...] = jnp.zeros(got.shape, F32)
        omegas[1] = jnp.zeros((8, 128), F32)

    @pl.when(jnp.logical_not(jnp.logical_or(odd & down, even & up)))
    def _():
        raw_far[...] = jnp.zeros((nx, ny), F32)

    def look_up(slot):
        pieces = [
            jnp.broadcast_to(levels[pl.ds(j * 128, 128)].reshape(1, 128), (nx, 128))
            for j in range(levels.shape[0] // 128)
        ]
        for h in range(ny // 128):
            cols = pl.ds(h * 128, 128)
            idx = index[slot, :, cols]
            inner = idx & 127
            value = jnp.take_along_axis(pieces[0], inner, axis=1, mode="promise_in_bounds")
            for j in range(1, len(pieces)):
                other = jnp.take_along_axis(pieces[j], inner, axis=1, mode="promise_in_bounds")
                value = jnp.where(idx >= j * 128, other, value)
            planes[slot, :, cols] = value
        columns = jnp.sum(planes[slot], axis=0, keepdims=True)
        return jnp.sum(columns, axis=1, keepdims=True) * (1.0 / (nx * ny))

    def phases(omega, mean_slow):
        q = (omega * mean_slow) ** 2 - wsq[...]
        root = jnp.sqrt(jnp.abs(q))
        sin_v, cos_v = sincos(root)
        moving = q > 0.0
        scale = 1.0 / (nx * ny)
        cos_p = jnp.where(moving, cos_v, jnp.exp(-root)) * scale
        sin_p = jnp.where(moving, sin_v, 0.0) * scale
        return cos_p, sin_p

    def screens(omega, slot, mean_slow):
        return sincos(omega * (planes[slot] - mean_slow))

    def spectral(source, which, phase):
        x_c, x_s, x_n = ((xs[i], xs[i + 3]) for i in range(3))
        y_c, y_s, y_n = ((ys[i], ys[i + 3]) for i in range(3))
        x_fwd = [block(x_c[i], x_s[i], x_n[i], x_c[i]) for i in (0, 1)]
        x_inv = [block(x_c[i], x_n[i], x_s[i], x_c[i]) for i in (0, 1)]
        y_fwd = [block(y_c[i], y_n[i], y_s[i], y_c[i]) for i in (0, 1)]
        y_inv = [block(y_c[i], y_s[i], y_n[i], y_c[i]) for i in (0, 1)]
        tw_c, tw_s = tw[:1], tw[1:2]
        cos_p, sin_p = phase
        mixed = []
        for f in which:
            spec = dot_data_right(*x_fwd, cat([source[f, 0], source[f, 1]], 0))
            left, right = spec[:, :half], spec[:, half:]
            plus, minus = left + right, left - right
            m_re, m_im = minus[:nx], minus[nx:]
            mixed.append(cat([
                cat([plus[:nx], plus[nx:]], 1),
                cat([m_re * tw_c + m_im * tw_s, m_im * tw_c - m_re * tw_s], 1),
            ], 0))
        spectrum = dot_data_left(cat(mixed, 0), *y_fwd)
        shifted = []
        for at, f in enumerate(which):
            v = spectrum[at * 2 * nx:(at + 1) * 2 * nx]
            v_re, v_im = v[:, :half], v[:, half:]
            if f == 0:
                shifted.append(cat([v_re * cos_p - v_im * sin_p, v_re * sin_p + v_im * cos_p], 1))
            else:
                shifted.append(cat([v_re * cos_p + v_im * sin_p, v_im * cos_p - v_re * sin_p], 1))
        back = dot_data_left(cat(shifted, 0), *y_inv)
        out = []
        for at, f in enumerate(which):
            b = back[at * 2 * nx:(at + 1) * 2 * nx]
            e_re, e_im = b[:nx, :half], b[:nx, half:]
            t_re, t_im = b[nx:, :half], b[nx:, half:]
            o_re, o_im = t_re * tw_c - t_im * tw_s, t_im * tw_c + t_re * tw_s
            moved = dot_data_right(*x_inv, cat([
                cat([e_re + o_re, e_re - o_re], 1), cat([e_im + o_im, e_im - o_im], 1),
            ], 0))
            out.append((moved[:nx], moved[nx:]))
        return out

    def turned(f, b_re, b_im, screen):
        s_sin, s_cos = screen
        if f == 0:
            return b_re * s_cos - b_im * s_sin, b_re * s_sin + b_im * s_cos
        return b_re * s_cos + b_im * s_sin, b_im * s_cos - b_re * s_sin

    def step(source, target, which, phase, screen):
        for f, (b_re, b_im) in zip(which, spectral(source, which, phase)):
            target[f, 0], target[f, 1] = turned(f, b_re, b_im, screen)

    def product(ref):
        return ref[0, 0] * ref[1, 0] + ref[0, 1] * ref[1, 1]

    def omega_of(slot):
        return omegas[slot, :1, :1]

    def remote(src, dst, send, recv, offset):
        return pltpu.make_async_remote_copy(
            src_ref=src, dst_ref=dst, send_sem=send, recv_sem=recv, device_id=to(offset)
        )

    def field_copy(f):
        return remote(made.at[f], got.at[f], far_send.at[f], far_recv.at[f], 2)

    def omega_copy():
        return remote(omegas.at[0], omegas.at[1], far_send.at[2], far_recv.at[2], 2)

    def mean_copy():
        return remote(means.at[0], means.at[1], far_send.at[3], far_recv.at[3], -2)

    def tile_copy(j):
        part = part_of(j)
        return remote(
            made.at[1, :, part], got.at[1, :, part], tile_send.at[j], tile_recv.at[j], 2
        )

    def index_copy(offset):
        return remote(sidx.at[0], index.at[1], pair_send.at[0], pair_recv.at[0], offset)

    def part_copy(offset):
        return remote(part_out, part_in, pair_send.at[1], pair_recv.at[1], offset)

    def near_copy(j, offset):
        part = part_of(j)
        return remote(raw_out.at[part], raw_near.at[part], near_send.at[j], near_recv.at[j], offset)

    def edge_copy(j, offset):
        part = part_of(j)
        return remote(raw_out.at[part], raw_far.at[part], edge_send.at[j], edge_recv.at[j], offset)

    def pass_copy():
        return remote(raw_near, raw_far, far_send.at[1], far_recv.at[1], 2)

    chunks = range(CHUNKS)

    @pl.when(odd)
    def _():
        for load in loads[:6]:
            load.wait()
        mean_own = look_up(0)
        phase = phases(omega_of(0), mean_own)
        screen_own = screens(omega_of(0), 0, mean_own)
        step(own, made, (0,), phase, screen_own)
        pl.semaphore_wait(barrier, 1 + jnp.where(down, 2, 0) + jnp.where(up, 1, 0))

        @pl.when(down)
        def _():
            omega_copy().start()
            field_copy(0).start()

        index_copy(-1).start()
        loads[6].wait()
        step(own, made, (1,), phase, screen_own)

        @pl.when(down)
        def _():
            field_copy(1).start()

        first[...] = product(made)
        index_copy(1).wait_recv()

        @pl.when(up)
        def _():
            omega_copy().wait_recv()

        mean_low = look_up(1)
        phase_0 = phases(omega_of(1), mean_low)
        screen_0 = screens(omega_of(1), 1, mean_low)
        phase_1 = phases(omega_of(1), mean_own)
        screen_1 = screens(omega_of(1), 0, mean_own)

        @pl.when(up)
        def _():
            field_copy(0).wait_recv()

        step(got, work, (0,), phase_0, screen_0)
        step(work, fields_out.at[0], (0,), phase_1, screen_1)

        @pl.when(up)
        def _():
            field_copy(1).wait_recv()

        step(got, work, (1,), phase_0, screen_0)
        part_out[...] = product(work)
        part_copy(-1).start()
        step(work, fields_out.at[0], (1,), phase_1, screen_1)
        part_copy(1).wait_recv()
        raw_out[...] = first[...] + part_in[...] + product(fields_out.at[0])
        for j in chunks:
            near_copy(j, -1).start()

        for j in chunks:
            part = part_of(j)
            near_copy(j, 1).wait_recv()

            @pl.when(down)
            def _():
                edge_copy(j, -1).wait_recv()

            image_out[0, part] = raw_out[part] - 0.25 * (raw_near[part] + raw_far[part])

        index_copy(-1).wait_send()
        part_copy(-1).wait_send()
        for j in chunks:
            near_copy(j, -1).wait_send()

        @pl.when(down)
        def _():
            omega_copy().wait_send()
            field_copy(0).wait_send()
            field_copy(1).wait_send()

    @pl.when(even)
    def _():
        for load in loads:
            load.wait()
        mean_own = look_up(0)
        means[0] = jnp.broadcast_to(mean_own, (8, 128))
        phase = phases(omega_of(0), mean_own)
        screen = screens(omega_of(0), 0, mean_own)
        step(own, work, (0, 1), phase, screen)
        first[...] = product(work)
        pl.semaphore_wait(barrier, 1 + jnp.where(down, 1, 0) + jnp.where(up, 2, 0))

        @pl.when(up)
        def _():
            mean_copy().start()

        @pl.when(down)
        def _():
            omega_copy().start()

        index_copy(1).start()
        index_copy(-1).wait_recv()
        mean_next = look_up(1)
        phase = phases(omega_of(0), mean_next)
        screen = screens(omega_of(0), 1, mean_next)
        step(work, own, (0, 1), phase, screen)
        part_out[...] = product(own)
        part_copy(1).start()

        @pl.when(down)
        def _():
            mean_copy().wait_recv()
            phase = phases(omega_of(0), means[1, :1, :1])
            made[0, 0], made[0, 1] = spectral(own, (0,), phase)[0]
            field_copy(0).start()
            made[1, 0], made[1, 1] = spectral(own, (1,), phase)[0]
            for j in chunks:
                tile_copy(j).start()

        @pl.when(up)
        def _():
            omega_copy().wait_recv()

        turns[0], turns[1] = screens(omega_of(1), 0, means[0, :1, :1])
        part_copy(-1).wait_recv()
        first[...] = first[...] + part_in[...]

        @pl.when(up)
        def _():
            field_copy(0).wait_recv()

        for j in chunks:
            part = part_of(j)
            if j == 1:
                for i in chunks:
                    near_copy(i, -1).wait_recv()

                @pl.when(down)
                def _():
                    field_copy(0).wait_send()
                    for i in range(1):
                        tile_copy(i).wait_send()
                    pass_copy().start()

            @pl.when(up)
            def _():
                tile_copy(j).wait_recv()

            screen = turns[0, part], turns[1, part]
            s_re, s_im = turned(0, got[0, 0, part], got[0, 1, part], screen)
            r_re, r_im = turned(1, got[1, 0, part], got[1, 1, part], screen)
            raw_out[part] = first[part] + s_re * r_re + s_im * r_im

            @pl.when(up)
            def _():
                edge_copy(j, -1).start()

            near_copy(j, 1).start()
            fields_out[0, 0, 0, part], fields_out[0, 0, 1, part] = s_re, s_im
            fields_out[0, 1, 0, part], fields_out[0, 1, 1, part] = r_re, r_im

        @pl.when(up)
        def _():
            pass_copy().wait_recv()

        image_out[0] = raw_out[...] - 0.25 * (raw_near[...] + raw_far[...])

        index_copy(1).wait_send()
        part_copy(1).wait_send()
        for j in chunks:
            near_copy(j, 1).wait_send()

        @pl.when(down)
        def _():
            omega_copy().wait_send()
            pass_copy().wait_send()
            for j in range(1, CHUNKS):
                tile_copy(j).wait_send()

        @pl.when(up)
        def _():
            mean_copy().wait_send()
            for j in chunks:
                edge_copy(j, -1).wait_send()


def store(image, fields, image_out, fields_out, sems):
    copies = [
        pltpu.make_async_copy(fields, fields_out, sems.at[0]),
        pltpu.make_async_copy(image, image_out, sems.at[1]),
    ]
    for copy in copies:
        copy.start()
    for copy in copies:
        copy.wait()


def body(fields, freq_index, slowness_index, slowness_table):
    nx, ny = slowness_index.shape[1:]
    count = lax.axis_size("slab")
    assert slowness_index.shape[0] == 1 and count % 2 == 0
    half = ny // 2
    xs, ys, tw = dft_table(nx), dft_table(half), twiddle_table(ny)
    any_spec = pl.BlockSpec(memory_space=pl.ANY)
    vmem_spec = pl.BlockSpec(memory_space=pltpu.VMEM)
    plane = (nx, ny)
    dma = pltpu.SemaphoreType.DMA
    image, moved = pl.pallas_call(
        functools.partial(kernel, count),
        out_shape=(pltpu.VMEM((1, nx, ny), F32), pltpu.VMEM(fields.shape, F32)),
        in_specs=[
            any_spec, pl.BlockSpec(memory_space=pltpu.SMEM), any_spec, any_spec,
            any_spec, any_spec, any_spec,
        ],
        out_specs=(vmem_spec, vmem_spec),
        scratch_shapes=[
            pltpu.VMEM((2, 2) + plane, F32),
            pltpu.VMEM((2, 2) + plane, F32),
            pltpu.VMEM((2, 2) + plane, F32),
            pltpu.VMEM((2, 2) + plane, F32),
            pltpu.VMEM((2,) + plane, jnp.int32),
            pltpu.VMEM((2,) + plane, F32),
            pltpu.VMEM(slowness_table.shape, F32),
            pltpu.VMEM(xs.shape, BF16),
            pltpu.VMEM(ys.shape, BF16),
            pltpu.VMEM(tw.shape, F32),
            pltpu.VMEM((2 * nx, half), F32),
            pltpu.VMEM((2, 8, 128), F32),
            pltpu.VMEM((2, 8, 128), F32),
            pltpu.VMEM((2,) + plane, F32),
            pltpu.VMEM(plane, F32),
            pltpu.VMEM(plane, F32),
            pltpu.VMEM(plane, F32),
            pltpu.VMEM(plane, F32),
            pltpu.VMEM(plane, F32),
            pltpu.VMEM(plane, F32),
            dma((7,)),
            dma((4,)),
            dma((4,)),
            dma((CHUNKS,)),
            dma((CHUNKS,)),
            dma((2,)),
            dma((2,)),
            dma((CHUNKS,)),
            dma((CHUNKS,)),
            dma((CHUNKS,)),
            dma((CHUNKS,)),
        ],
        compiler_params=pltpu.CompilerParams(collective_id=0, has_side_effects=True),
        name="slabs",
    )(
        fields, freq_index, slowness_index, slowness_table,
        jnp.asarray(xs), jnp.asarray(ys), jnp.asarray(tw),
    )
    return pl.pallas_call(
        store,
        out_shape=(
            jax.ShapeDtypeStruct((1, nx, ny), F32),
            jax.ShapeDtypeStruct(fields.shape, F32),
        ),
        in_specs=[vmem_spec, vmem_spec],
        out_specs=(any_spec, any_spec),
        scratch_shapes=[dma((2,))],
        name="store",
    )(
        pltpu.with_memory_space_constraint(image, pltpu.VMEM),
        pltpu.with_memory_space_constraint(moved, pltpu.VMEM),
    )


def solution(mesh):
    return jax.shard_map(
        body,
        mesh=mesh,
        in_specs=(
            P(("shots", "slab"), None, None, None, None),
            P(("shots", "slab")),
            P("slab", None, None),
            P(),
        ),
        out_specs=(P(("shots", "slab"), None, None), P(("shots", "slab"), None, None, None, None)),
        check_vma=False,
    )
```

```python
import functools
import math

import jax
import jax.numpy as jnp
import numpy as np
from jax import lax
from jax.experimental import pallas as pl
from jax.experimental.pallas import tpu as pltpu
from jax.sharding import PartitionSpec as P

NFREQ = 512
SHARES = (3, 2, 2, 1)
CHUNKS = len(SHARES)

F32 = jnp.float32
BF16 = jnp.bfloat16
PI_HI = 3.140625
PI_LO = math.pi - 3.140625


def dft_table(n):
    turn = np.outer(np.arange(n), np.arange(n)) % n * (2.0 * np.pi / n)
    mats = [np.cos(turn), np.sin(turn), -np.sin(turn)]
    high = [mat.astype(BF16) for mat in mats]
    low = [(mat - h.astype(np.float64)).astype(BF16) for mat, h in zip(mats, high)]
    return np.stack(high + low)


def twiddle_table(ny):
    turn = np.arange(ny // 2) * (2.0 * np.pi / ny)
    rows = np.zeros((8, ny // 2), np.float32)
    rows[0], rows[1] = np.cos(turn), np.sin(turn)
    return rows


def split(value):
    high = value.astype(BF16)
    low = (value - high.astype(F32)).astype(BF16)
    return high, low


def cat(values, axis):
    return jnp.concatenate(values, axis=axis)


def block(a, b, c, d):
    return cat([cat([a, b], 1), cat([c, d], 1)], 0)


def dot_data_left(data, high, low):
    d_high, d_low = split(data)
    return jnp.dot(cat([d_high, d_low, d_high], 1), cat([high, high, low], 0), preferred_element_type=F32)


def dot_data_right(high, low, data):
    d_high, d_low = split(data)
    return jnp.dot(cat([high, high, low], 1), cat([d_high, d_low, d_high], 0), preferred_element_type=F32)


def sincos(x):
    turns = jnp.floor(x * (1.0 / math.pi) + 0.5)
    r = (x - turns * PI_HI) - turns * PI_LO
    sign = 1.0 - 2.0 * (turns - 2.0 * jnp.floor(turns * 0.5))
    r2 = r * r
    sin_p = 1.0 / math.factorial(11) * -1.0
    for k, sg in ((9, 1.0), (7, -1.0), (5, 1.0), (3, -1.0)):
        sin_p = sin_p * r2 + sg / math.factorial(k)
    sin_p = r + r * (r2 * sin_p)
    cos_p = 1.0 / math.factorial(12)
    for k, sg in ((10, -1.0), (8, 1.0), (6, -1.0), (4, 1.0), (2, -1.0), (0, 1.0)):
        cos_p = cos_p * r2 + sg / math.factorial(k)
    return sign * sin_p, sign * cos_p


def kernel(
    count, fields, freq, sidx, table, xs_in, ys_in, tw_in, image_out, fields_out,
    own, work, made, got, index, planes, levels, xs, ys, tw, wsq, omegas, means, turns,
    part_out, part_in, raw_out, raw_near, raw_far, first,
    in_sems, far_send, far_recv, tile_send, tile_recv, pair_send, pair_recv,
    near_send, near_recv, edge_send, edge_recv,
):
    me = lax.axis_index("slab")
    nx, ny = index.shape[1:]
    half = ny // 2
    unit = nx // sum(SHARES)
    starts = [unit * sum(SHARES[:j]) for j in range(CHUNKS)]

    def part_of(j):
        return pl.ds(starts[j], unit * SHARES[j])

    odd = lax.rem(me, 2) == 1
    even = jnp.logical_not(odd)
    down = me + 2 < count
    up = me >= 2

    def to(offset):
        return {"slab": jnp.clip(me + offset, 0, count - 1)}

    loads = [
        pltpu.make_async_copy(fields.at[0, 0], own.at[0], in_sems.at[0]),
        pltpu.make_async_copy(xs_in, xs, in_sems.at[1]),
        pltpu.make_async_copy(table, levels, in_sems.at[2]),
        pltpu.make_async_copy(sidx.at[0], index.at[0], in_sems.at[3]),
        pltpu.make_async_copy(ys_in, ys, in_sems.at[4]),
        pltpu.make_async_copy(tw_in, tw, in_sems.at[5]),
        pltpu.make_async_copy(fields.at[0, 1], own.at[1], in_sems.at[6]),
    ]
    for load in loads:
        load.start()

    barrier = pltpu.get_barrier_semaphore()

    @pl.when(odd)
    def _():
        pl.semaphore_signal(barrier, inc=1, device_id=to(-1))

        @pl.when(down)
        def _():
            pl.semaphore_signal(barrier, inc=1, device_id=to(1))

    @pl.when(even)
    def _():
        pl.semaphore_signal(barrier, inc=1, device_id=to(1))

        @pl.when(up)
        def _():
            pl.semaphore_signal(barrier, inc=1, device_id=to(-1))

    @pl.when(down)
    def _():
        pl.semaphore_signal(barrier, inc=1, device_id=to(2))

    @pl.when(up)
    def _():
        pl.semaphore_signal(barrier, inc=1, device_id=to(-2))

    row = lax.broadcasted_iota(jnp.int32, (nx, half), 0)
    wave_x = jnp.where(row < (nx + 1) // 2, row, row - nx).astype(F32) * (2.0 * math.pi / nx)
    lane = lax.broadcasted_iota(jnp.int32, (1, half), 1)
    for parity in (0, 1):
        k = 2 * lane + parity
        wave_y = jnp.where(k < (ny + 1) // 2, k, k - ny).astype(F32) * (2.0 * math.pi / ny)
        wsq[pl.ds(parity * nx, nx)] = wave_x * wave_x + wave_y * wave_y

    omegas[0] = jnp.full((8, 128), 1.0 + freq[0].astype(F32) / NFREQ, F32)

    @pl.when(jnp.logical_not(up))
    def _():
        got[...] = jnp.zeros(got.shape, F32)
        omegas[1] = jnp.zeros((8, 128), F32)

    @pl.when(jnp.logical_not(jnp.logical_or(odd & down, even & up)))
    def _():
        raw_far[...] = jnp.zeros((nx, ny), F32)

    def look_up(slot):
        pieces = [
            jnp.broadcast_to(levels[pl.ds(j * 128, 128)].reshape(1, 128), (nx, 128))
            for j in range(levels.shape[0] // 128)
        ]
        for h in range(ny // 128):
            cols = pl.ds(h * 128, 128)
            idx = index[slot, :, cols]
            inner = idx & 127
            value = jnp.take_along_axis(pieces[0], inner, axis=1, mode="promise_in_bounds")
            for j in range(1, len(pieces)):
                other = jnp.take_along_axis(pieces[j], inner, axis=1, mode="promise_in_bounds")
                value = jnp.where(idx >= j * 128, other, value)
            planes[slot, :, cols] = value
        columns = jnp.sum(planes[slot], axis=0, keepdims=True)
        return jnp.sum(columns, axis=1, keepdims=True) * (1.0 / (nx * ny))

    def phases(omega, mean_slow):
        q = (omega * mean_slow) ** 2 - wsq[...]
        root = jnp.sqrt(jnp.abs(q))
        sin_v, cos_v = sincos(root)
        moving = q > 0.0
        scale = 1.0 / (nx * ny)
        cos_p = jnp.where(moving, cos_v, jnp.exp(-root)) * scale
        sin_p = jnp.where(moving, sin_v, 0.0) * scale
        return cos_p, sin_p

    def screens(omega, slot, mean_slow):
        return sincos(omega * (planes[slot] - mean_slow))

    def spectral(source, which, phase):
        x_c, x_s, x_n = ((xs[i], xs[i + 3]) for i in range(3))
        y_c, y_s, y_n = ((ys[i], ys[i + 3]) for i in range(3))
        x_fwd = [block(x_c[i], x_s[i], x_n[i], x_c[i]) for i in (0, 1)]
        x_inv = [block(x_c[i], x_n[i], x_s[i], x_c[i]) for i in (0, 1)]
        y_fwd = [block(y_c[i], y_n[i], y_s[i], y_c[i]) for i in (0, 1)]
        y_inv = [block(y_c[i], y_s[i], y_n[i], y_c[i]) for i in (0, 1)]
        tw_c, tw_s = tw[:1], tw[1:2]
        cos_p, sin_p = phase
        mixed = []
        for f in which:
            spec = dot_data_right(*x_fwd, cat([source[f, 0], source[f, 1]], 0))
            left, right = spec[:, :half], spec[:, half:]
            plus, minus = left + right, left - right
            m_re, m_im = minus[:nx], minus[nx:]
            mixed.append(cat([
                cat([plus[:nx], plus[nx:]], 1),
                cat([m_re * tw_c + m_im * tw_s, m_im * tw_c - m_re * tw_s], 1),
            ], 0))
        spectrum = dot_data_left(cat(mixed, 0), *y_fwd)
        shifted = []
        for at, f in enumerate(which):
            v = spectrum[at * 2 * nx:(at + 1) * 2 * nx]
            v_re, v_im = v[:, :half], v[:, half:]
            if f == 0:
                shifted.append(cat([v_re * cos_p - v_im * sin_p, v_re * sin_p + v_im * cos_p], 1))
            else:
                shifted.append(cat([v_re * cos_p + v_im * sin_p, v_im * cos_p - v_re * sin_p], 1))
        back = dot_data_left(cat(shifted, 0), *y_inv)
        out = []
        for at, f in enumerate(which):
            b = back[at * 2 * nx:(at + 1) * 2 * nx]
            e_re, e_im = b[:nx, :half], b[:nx, half:]
            t_re, t_im = b[nx:, :half], b[nx:, half:]
            o_re, o_im = t_re * tw_c - t_im * tw_s, t_im * tw_c + t_re * tw_s
            moved = dot_data_right(*x_inv, cat([
                cat([e_re + o_re, e_re - o_re], 1), cat([e_im + o_im, e_im - o_im], 1),
            ], 0))
            out.append((moved[:nx], moved[nx:]))
        return out

    def turned(f, b_re, b_im, screen):
        s_sin, s_cos = screen
        if f == 0:
            return b_re * s_cos - b_im * s_sin, b_re * s_sin + b_im * s_cos
        return b_re * s_cos + b_im * s_sin, b_im * s_cos - b_re * s_sin

    def step(source, target, which, phase, screen):
        for f, (b_re, b_im) in zip(which, spectral(source, which, phase)):
            target[f, 0], target[f, 1] = turned(f, b_re, b_im, screen)

    def product(ref):
        return ref[0, 0] * ref[1, 0] + ref[0, 1] * ref[1, 1]

    def omega_of(slot):
        return omegas[slot, :1, :1]

    def remote(src, dst, send, recv, offset):
        return pltpu.make_async_remote_copy(
            src_ref=src, dst_ref=dst, send_sem=send, recv_sem=recv, device_id=to(offset)
        )

    def field_copy(f):
        return remote(made.at[f], got.at[f], far_send.at[f], far_recv.at[f], 2)

    def omega_copy():
        return remote(omegas.at[0], omegas.at[1], far_send.at[2], far_recv.at[2], 2)

    def mean_copy():
        return remote(means.at[0], means.at[1], far_send.at[3], far_recv.at[3], -2)

    def tile_copy(j):
        part = part_of(j)
        return remote(
            made.at[1, :, part], got.at[1, :, part], tile_send.at[j], tile_recv.at[j], 2
        )

    def index_copy(offset):
        return remote(sidx.at[0], index.at[1], pair_send.at[0], pair_recv.at[0], offset)

    def part_copy(offset):
        return remote(part_out, part_in, pair_send.at[1], pair_recv.at[1], offset)

    def near_copy(j, offset):
        part = part_of(j)
        return remote(raw_out.at[part], raw_near.at[part], near_send.at[j], near_recv.at[j], offset)

    def edge_copy(j, offset):
        part = part_of(j)
        return remote(raw_out.at[part], raw_far.at[part], edge_send.at[j], edge_recv.at[j], offset)

    def pass_copy():
        return remote(raw_near, raw_far, far_send.at[1], far_recv.at[1], 2)

    chunks = range(CHUNKS)

    @pl.when(odd)
    def _():
        for load in loads[:6]:
            load.wait()
        mean_own = look_up(0)
        phase = phases(omega_of(0), mean_own)
        screen_own = screens(omega_of(0), 0, mean_own)
        step(own, made, (0,), phase, screen_own)
        pl.semaphore_wait(barrier, 1 + jnp.where(down, 2, 0) + jnp.where(up, 1, 0))

        @pl.when(down)
        def _():
            omega_copy().start()
            field_copy(0).start()

        index_copy(-1).start()
        loads[6].wait()
        step(own, made, (1,), phase, screen_own)

        @pl.when(down)
        def _():
            field_copy(1).start()

        first[...] = product(made)
        index_copy(1).wait_recv()

        @pl.when(up)
        def _():
            omega_copy().wait_recv()

        mean_low = look_up(1)
        phase_0 = phases(omega_of(1), mean_low)
        screen_0 = screens(omega_of(1), 1, mean_low)
        phase_1 = phases(omega_of(1), mean_own)
        screen_1 = screens(omega_of(1), 0, mean_own)

        @pl.when(up)
        def _():
            field_copy(0).wait_recv()

        step(got, work, (0,), phase_0, screen_0)
        step(work, fields_out.at[0], (0,), phase_1, screen_1)

        @pl.when(up)
        def _():
            field_copy(1).wait_recv()

        step(got, work, (1,), phase_0, screen_0)
        part_out[...] = product(work)
        part_copy(-1).start()
        step(work, fields_out.at[0], (1,), phase_1, screen_1)
        part_copy(1).wait_recv()
        raw_out[...] = first[...] + part_in[...] + product(fields_out.at[0])
        for j in chunks:
            near_copy(j, -1).start()

        for j in chunks:
            part = part_of(j)
            near_copy(j, 1).wait_recv()

            @pl.when(down)
            def _():
                edge_copy(j, -1).wait_recv()

            image_out[0, part] = raw_out[part] - 0.25 * (raw_near[part] + raw_far[part])

        index_copy(-1).wait_send()
        part_copy(-1).wait_send()
        for j in chunks:
            near_copy(j, -1).wait_send()

        @pl.when(down)
        def _():
            omega_copy().wait_send()
            field_copy(0).wait_send()
            field_copy(1).wait_send()

    @pl.when(even)
    def _():
        for load in loads:
            load.wait()
        mean_own = look_up(0)
        means[0] = jnp.broadcast_to(mean_own, (8, 128))
        pl.semaphore_wait(barrier, 1 + jnp.where(down, 1, 0) + jnp.where(up, 2, 0))

        @pl.when(up)
        def _():
            mean_copy().start()

        @pl.when(down)
        def _():
            omega_copy().start()

        index_copy(1).start()
        phase = phases(omega_of(0), mean_own)
        screen = screens(omega_of(0), 0, mean_own)
        step(own, work, (0, 1), phase, screen)
        first[...] = product(work)
        index_copy(-1).wait_recv()
        mean_next = look_up(1)
        phase = phases(omega_of(0), mean_next)
        screen = screens(omega_of(0), 1, mean_next)
        step(work, own, (0, 1), phase, screen)
        part_out[...] = product(own)
        part_copy(1).start()

        @pl.when(down)
        def _():
            mean_copy().wait_recv()
            phase = phases(omega_of(0), means[1, :1, :1])
            made[0, 0], made[0, 1] = spectral(own, (0,), phase)[0]
            field_copy(0).start()
            made[1, 0], made[1, 1] = spectral(own, (1,), phase)[0]
            for j in chunks:
                tile_copy(j).start()

        @pl.when(up)
        def _():
            omega_copy().wait_recv()

        turns[0], turns[1] = screens(omega_of(1), 0, means[0, :1, :1])
        part_copy(-1).wait_recv()
        first[...] = first[...] + part_in[...]

        @pl.when(up)
        def _():
            field_copy(0).wait_recv()

        for j in chunks:
            part = part_of(j)
            if j == 1:
                for i in chunks:
                    near_copy(i, -1).wait_recv()

                @pl.when(down)
                def _():
                    field_copy(0).wait_send()
                    for i in range(1):
                        tile_copy(i).wait_send()
                    pass_copy().start()

            @pl.when(up)
            def _():
                tile_copy(j).wait_recv()

            screen = turns[0, part], turns[1, part]
            s_re, s_im = turned(0, got[0, 0, part], got[0, 1, part], screen)
            r_re, r_im = turned(1, got[1, 0, part], got[1, 1, part], screen)
            raw_out[part] = first[part] + s_re * r_re + s_im * r_im

            @pl.when(up)
            def _():
                edge_copy(j, -1).start()

            near_copy(j, 1).start()
            fields_out[0, 0, 0, part], fields_out[0, 0, 1, part] = s_re, s_im
            fields_out[0, 1, 0, part], fields_out[0, 1, 1, part] = r_re, r_im

        @pl.when(up)
        def _():
            pass_copy().wait_recv()

        image_out[0] = raw_out[...] - 0.25 * (raw_near[...] + raw_far[...])

        index_copy(1).wait_send()
        part_copy(1).wait_send()
        for j in chunks:
            near_copy(j, 1).wait_send()

        @pl.when(down)
        def _():
            omega_copy().wait_send()
            pass_copy().wait_send()
            for j in range(1, CHUNKS):
                tile_copy(j).wait_send()

        @pl.when(up)
        def _():
            mean_copy().wait_send()
            for j in chunks:
                edge_copy(j, -1).wait_send()


def store(image, fields, image_out, fields_out, sems):
    copies = [
        pltpu.make_async_copy(fields, fields_out, sems.at[0]),
        pltpu.make_async_copy(image, image_out, sems.at[1]),
    ]
    for copy in copies:
        copy.start()
    for copy in copies:
        copy.wait()


def body(fields, freq_index, slowness_index, slowness_table):
    nx, ny = slowness_index.shape[1:]
    count = lax.axis_size("slab")
    assert slowness_index.shape[0] == 1 and count % 2 == 0
    half = ny // 2
    xs, ys, tw = dft_table(nx), dft_table(half), twiddle_table(ny)
    any_spec = pl.BlockSpec(memory_space=pl.ANY)
    vmem_spec = pl.BlockSpec(memory_space=pltpu.VMEM)
    plane = (nx, ny)
    dma = pltpu.SemaphoreType.DMA
    image, moved = pl.pallas_call(
        functools.partial(kernel, count),
        out_shape=(pltpu.VMEM((1, nx, ny), F32), pltpu.VMEM(fields.shape, F32)),
        in_specs=[
            any_spec, pl.BlockSpec(memory_space=pltpu.SMEM), any_spec, any_spec,
            any_spec, any_spec, any_spec,
        ],
        out_specs=(vmem_spec, vmem_spec),
        scratch_shapes=[
            pltpu.VMEM((2, 2) + plane, F32),
            pltpu.VMEM((2, 2) + plane, F32),
            pltpu.VMEM((2, 2) + plane, F32),
            pltpu.VMEM((2, 2) + plane, F32),
            pltpu.VMEM((2,) + plane, jnp.int32),
            pltpu.VMEM((2,) + plane, F32),
            pltpu.VMEM(slowness_table.shape, F32),
            pltpu.VMEM(xs.shape, BF16),
            pltpu.VMEM(ys.shape, BF16),
            pltpu.VMEM(tw.shape, F32),
            pltpu.VMEM((2 * nx, half), F32),
            pltpu.VMEM((2, 8, 128), F32),
            pltpu.VMEM((2, 8, 128), F32),
            pltpu.VMEM((2,) + plane, F32),
            pltpu.VMEM(plane, F32),
            pltpu.VMEM(plane, F32),
            pltpu.VMEM(plane, F32),
            pltpu.VMEM(plane, F32),
            pltpu.VMEM(plane, F32),
            pltpu.VMEM(plane, F32),
            dma((7,)),
            dma((4,)),
            dma((4,)),
            dma((CHUNKS,)),
            dma((CHUNKS,)),
            dma((2,)),
            dma((2,)),
            dma((CHUNKS,)),
            dma((CHUNKS,)),
            dma((CHUNKS,)),
            dma((CHUNKS,)),
        ],
        compiler_params=pltpu.CompilerParams(collective_id=0, has_side_effects=True),
        name="slabs",
    )(
        fields, freq_index, slowness_index, slowness_table,
        jnp.asarray(xs), jnp.asarray(ys), jnp.asarray(tw),
    )
    return pl.pallas_call(
        store,
        out_shape=(
            jax.ShapeDtypeStruct((1, nx, ny), F32),
            jax.ShapeDtypeStruct(fields.shape, F32),
        ),
        in_specs=[vmem_spec, vmem_spec],
        out_specs=(any_spec, any_spec),
        scratch_shapes=[dma((2,))],
        name="store",
    )(
        pltpu.with_memory_space_constraint(image, pltpu.VMEM),
        pltpu.with_memory_space_constraint(moved, pltpu.VMEM),
    )


def solution(mesh):
    return jax.shard_map(
        body,
        mesh=mesh,
        in_specs=(
            P(("shots", "slab"), None, None, None, None),
            P(("shots", "slab")),
            P("slab", None, None),
            P(),
        ),
        out_specs=(P(("shots", "slab"), None, None), P(("shots", "slab"), None, None, None, None)),
        check_vma=False,
    )
```

```python
import functools
import math

import jax
import jax.numpy as jnp
import numpy as np
from jax import lax
from jax.experimental import pallas as pl
from jax.experimental.pallas import tpu as pltpu
from jax.sharding import PartitionSpec as P

NFREQ = 512
SHARES = (3, 2, 2, 1)
CHUNKS = len(SHARES)

F32 = jnp.float32
BF16 = jnp.bfloat16
PI_HI = 3.140625
PI_LO = math.pi - 3.140625


def dft_table(n):
    turn = np.outer(np.arange(n), np.arange(n)) % n * (2.0 * np.pi / n)
    mats = [np.cos(turn), np.sin(turn), -np.sin(turn)]
    high = [mat.astype(BF16) for mat in mats]
    low = [(mat - h.astype(np.float64)).astype(BF16) for mat, h in zip(mats, high)]
    return np.stack(high + low)


def twiddle_table(ny):
    turn = np.arange(ny // 2) * (2.0 * np.pi / ny)
    rows = np.zeros((8, ny // 2), np.float32)
    rows[0], rows[1] = np.cos(turn), np.sin(turn)
    return rows


def split(value):
    high = value.astype(BF16)
    low = (value - high.astype(F32)).astype(BF16)
    return high, low


def cat(values, axis):
    return jnp.concatenate(values, axis=axis)


def block(a, b, c, d):
    return cat([cat([a, b], 1), cat([c, d], 1)], 0)


def dot_data_left(data, high, low):
    d_high, d_low = split(data)
    return jnp.dot(cat([d_high, d_low, d_high], 1), cat([high, high, low], 0), preferred_element_type=F32)


def dot_data_right(high, low, data):
    d_high, d_low = split(data)
    return jnp.dot(cat([high, high, low], 1), cat([d_high, d_low, d_high], 0), preferred_element_type=F32)


def sincos(x):
    turns = jnp.floor(x * (1.0 / math.pi) + 0.5)
    r = (x - turns * PI_HI) - turns * PI_LO
    sign = 1.0 - 2.0 * (turns - 2.0 * jnp.floor(turns * 0.5))
    r2 = r * r
    sin_p = 1.0 / math.factorial(11) * -1.0
    for k, sg in ((9, 1.0), (7, -1.0), (5, 1.0), (3, -1.0)):
        sin_p = sin_p * r2 + sg / math.factorial(k)
    sin_p = r + r * (r2 * sin_p)
    cos_p = 1.0 / math.factorial(12)
    for k, sg in ((10, -1.0), (8, 1.0), (6, -1.0), (4, 1.0), (2, -1.0), (0, 1.0)):
        cos_p = cos_p * r2 + sg / math.factorial(k)
    return sign * sin_p, sign * cos_p


def kernel(
    count, fields, freq, sidx, table, xs_in, ys_in, tw_in, image_out, fields_out,
    own, work, made, got, index, planes, levels, xs, ys, tw, wsq, omegas, means, turns,
    part_out, part_in, raw_out, raw_near, raw_far, first,
    in_sems, far_send, far_recv, tile_send, tile_recv, pair_send, pair_recv,
    near_send, near_recv, edge_send, edge_recv,
):
    me = lax.axis_index("slab")
    nx, ny = index.shape[1:]
    half = ny // 2
    unit = nx // sum(SHARES)
    starts = [unit * sum(SHARES[:j]) for j in range(CHUNKS)]

    def part_of(j):
        return pl.ds(starts[j], unit * SHARES[j])

    odd = lax.rem(me, 2) == 1
    even = jnp.logical_not(odd)
    down = me + 2 < count
    up = me >= 2
    straight = jnp.logical_and(up, lax.rem(me // 2, 2) == 0)

    def to(offset):
        return {"slab": jnp.clip(me + offset, 0, count - 1)}

    loads = [
        pltpu.make_async_copy(fields.at[0, 0], own.at[0], in_sems.at[0]),
        pltpu.make_async_copy(xs_in, xs, in_sems.at[1]),
        pltpu.make_async_copy(table, levels, in_sems.at[2]),
        pltpu.make_async_copy(sidx.at[0], index.at[0], in_sems.at[3]),
        pltpu.make_async_copy(ys_in, ys, in_sems.at[4]),
        pltpu.make_async_copy(tw_in, tw, in_sems.at[5]),
        pltpu.make_async_copy(fields.at[0, 1], own.at[1], in_sems.at[6]),
    ]
    for load in loads:
        load.start()

    barrier = pltpu.get_barrier_semaphore()

    @pl.when(odd)
    def _():
        pl.semaphore_signal(barrier, inc=1, device_id=to(-1))

        @pl.when(down)
        def _():
            pl.semaphore_signal(barrier, inc=1, device_id=to(1))

    @pl.when(even)
    def _():
        pl.semaphore_signal(barrier, inc=1, device_id=to(1))

        @pl.when(up)
        def _():
            pl.semaphore_signal(barrier, inc=1, device_id=to(-1))

    @pl.when(down)
    def _():
        pl.semaphore_signal(barrier, inc=1, device_id=to(2))

    @pl.when(up)
    def _():
        pl.semaphore_signal(barrier, inc=1, device_id=to(-2))

    row = lax.broadcasted_iota(jnp.int32, (nx, half), 0)
    wave_x = jnp.where(row < (nx + 1) // 2, row, row - nx).astype(F32) * (2.0 * math.pi / nx)
    lane = lax.broadcasted_iota(jnp.int32, (1, half), 1)
    for parity in (0, 1):
        k = 2 * lane + parity
        wave_y = jnp.where(k < (ny + 1) // 2, k, k - ny).astype(F32) * (2.0 * math.pi / ny)
        wsq[pl.ds(parity * nx, nx)] = wave_x * wave_x + wave_y * wave_y

    omegas[0] = jnp.full((8, 128), 1.0 + freq[0].astype(F32) / NFREQ, F32)

    @pl.when(jnp.logical_not(up))
    def _():
        got[...] = jnp.zeros(got.shape, F32)
        omegas[1] = jnp.zeros((8, 128), F32)

    @pl.when(jnp.logical_not(jnp.logical_or(odd & down, even & up)))
    def _():
        raw_far[...] = jnp.zeros((nx, ny), F32)

    def look_up(slot):
        pieces = [
            jnp.broadcast_to(levels[pl.ds(j * 128, 128)].reshape(1, 128), (nx, 128))
            for j in range(levels.shape[0] // 128)
        ]
        for h in range(ny // 128):
            cols = pl.ds(h * 128, 128)
            idx = index[slot, :, cols]
            inner = idx & 127
            value = jnp.take_along_axis(pieces[0], inner, axis=1, mode="promise_in_bounds")
            for j in range(1, len(pieces)):
                other = jnp.take_along_axis(pieces[j], inner, axis=1, mode="promise_in_bounds")
                value = jnp.where(idx >= j * 128, other, value)
            planes[slot, :, cols] = value
        columns = jnp.sum(planes[slot], axis=0, keepdims=True)
        return jnp.sum(columns, axis=1, keepdims=True) * (1.0 / (nx * ny))

    def phases(omega, mean_slow):
        q = (omega * mean_slow) ** 2 - wsq[...]
        root = jnp.sqrt(jnp.abs(q))
        sin_v, cos_v = sincos(root)
        moving = q > 0.0
        scale = 1.0 / (nx * ny)
        cos_p = jnp.where(moving, cos_v, jnp.exp(-root)) * scale
        sin_p = jnp.where(moving, sin_v, 0.0) * scale
        return cos_p, sin_p

    def screens(omega, slot, mean_slow):
        return sincos(omega * (planes[slot] - mean_slow))

    def spectral(source, which, phase):
        x_c, x_s, x_n = ((xs[i], xs[i + 3]) for i in range(3))
        y_c, y_s, y_n = ((ys[i], ys[i + 3]) for i in range(3))
        x_fwd = [block(x_c[i], x_s[i], x_n[i], x_c[i]) for i in (0, 1)]
        x_inv = [block(x_c[i], x_n[i], x_s[i], x_c[i]) for i in (0, 1)]
        y_fwd = [block(y_c[i], y_n[i], y_s[i], y_c[i]) for i in (0, 1)]
        y_inv = [block(y_c[i], y_s[i], y_n[i], y_c[i]) for i in (0, 1)]
        tw_c, tw_s = tw[:1], tw[1:2]
        cos_p, sin_p = phase
        mixed = []
        for f in which:
            spec = dot_data_right(*x_fwd, cat([source[f, 0], source[f, 1]], 0))
            left, right = spec[:, :half], spec[:, half:]
            plus, minus = left + right, left - right
            m_re, m_im = minus[:nx], minus[nx:]
            mixed.append(cat([
                cat([plus[:nx], plus[nx:]], 1),
                cat([m_re * tw_c + m_im * tw_s, m_im * tw_c - m_re * tw_s], 1),
            ], 0))
        spectrum = dot_data_left(cat(mixed, 0), *y_fwd)
        shifted = []
        for at, f in enumerate(which):
            v = spectrum[at * 2 * nx:(at + 1) * 2 * nx]
            v_re, v_im = v[:, :half], v[:, half:]
            if f == 0:
                shifted.append(cat([v_re * cos_p - v_im * sin_p, v_re * sin_p + v_im * cos_p], 1))
            else:
                shifted.append(cat([v_re * cos_p + v_im * sin_p, v_im * cos_p - v_re * sin_p], 1))
        back = dot_data_left(cat(shifted, 0), *y_inv)
        out = []
        for at, f in enumerate(which):
            b = back[at * 2 * nx:(at + 1) * 2 * nx]
            e_re, e_im = b[:nx, :half], b[:nx, half:]
            t_re, t_im = b[nx:, :half], b[nx:, half:]
            o_re, o_im = t_re * tw_c - t_im * tw_s, t_im * tw_c + t_re * tw_s
            moved = dot_data_right(*x_inv, cat([
                cat([e_re + o_re, e_re - o_re], 1), cat([e_im + o_im, e_im - o_im], 1),
            ], 0))
            out.append((moved[:nx], moved[nx:]))
        return out

    def turned(f, b_re, b_im, screen):
        s_sin, s_cos = screen
        if f == 0:
            return b_re * s_cos - b_im * s_sin, b_re * s_sin + b_im * s_cos
        return b_re * s_cos + b_im * s_sin, b_im * s_cos - b_re * s_sin

    def step(source, target, which, phase, screen):
        for f, (b_re, b_im) in zip(which, spectral(source, which, phase)):
            target[f, 0], target[f, 1] = turned(f, b_re, b_im, screen)

    def product(ref):
        return ref[0, 0] * ref[1, 0] + ref[0, 1] * ref[1, 1]

    def omega_of(slot):
        return omegas[slot, :1, :1]

    def remote(src, dst, send, recv, offset):
        return pltpu.make_async_remote_copy(
            src_ref=src, dst_ref=dst, send_sem=send, recv_sem=recv, device_id=to(offset)
        )

    def field_copy(f):
        return remote(made.at[f], got.at[f], far_send.at[f], far_recv.at[f], 2)

    def omega_copy():
        return remote(omegas.at[0], omegas.at[1], far_send.at[2], far_recv.at[2], 2)

    def mean_copy():
        return remote(means.at[0], means.at[1], far_send.at[3], far_recv.at[3], -2)

    def tile_copy(j):
        part = part_of(j)
        return remote(
            made.at[1, :, part], got.at[1, :, part], tile_send.at[j], tile_recv.at[j], 2
        )

    def index_copy(offset):
        return remote(sidx.at[0], index.at[1], pair_send.at[0], pair_recv.at[0], offset)

    def part_copy(offset):
        return remote(part_out, part_in, pair_send.at[1], pair_recv.at[1], offset)

    def near_copy(j, offset):
        part = part_of(j)
        return remote(raw_out.at[part], raw_near.at[part], near_send.at[j], near_recv.at[j], offset)

    def edge_copy(j, offset):
        part = part_of(j)
        return remote(raw_out.at[part], raw_far.at[part], edge_send.at[j], edge_recv.at[j], offset)

    def pass_copy(source, offset):
        return remote(source, raw_far, far_send.at[4], far_recv.at[4], offset)

    chunks = range(CHUNKS)

    @pl.when(odd)
    def _():
        for load in loads[:6]:
            load.wait()
        mean_own = look_up(0)
        phase = phases(omega_of(0), mean_own)
        screen_own = screens(omega_of(0), 0, mean_own)
        step(own, made, (0,), phase, screen_own)
        pl.semaphore_wait(barrier, 1 + jnp.where(down, 2, 0) + jnp.where(up, 1, 0))

        @pl.when(down)
        def _():
            omega_copy().start()
            field_copy(0).start()

        index_copy(-1).start()
        loads[6].wait()
        step(own, made, (1,), phase, screen_own)

        @pl.when(down)
        def _():
            field_copy(1).start()

        first[...] = product(made)
        index_copy(1).wait_recv()

        @pl.when(up)
        def _():
            omega_copy().wait_recv()

        mean_low = look_up(1)
        phase_0 = phases(omega_of(1), mean_low)
        screen_0 = screens(omega_of(1), 1, mean_low)
        phase_1 = phases(omega_of(1), mean_own)
        screen_1 = screens(omega_of(1), 0, mean_own)

        @pl.when(up)
        def _():
            field_copy(0).wait_recv()

        step(got, work, (0,), phase_0, screen_0)
        step(work, fields_out.at[0], (0,), phase_1, screen_1)

        @pl.when(up)
        def _():
            field_copy(1).wait_recv()

        step(got, work, (1,), phase_0, screen_0)
        part_out[...] = product(work)
        part_copy(-1).start()
        step(work, fields_out.at[0], (1,), phase_1, screen_1)
        part_copy(1).wait_recv()
        raw_out[...] = first[...] + part_in[...] + product(fields_out.at[0])
        @pl.when(jnp.logical_and(down, straight))
        def _():
            pass_copy(raw_out, 1).start()

        for j in chunks:
            near_copy(j, -1).start()

        for j in chunks:
            part = part_of(j)
            near_copy(j, 1).wait_recv()

            @pl.when(down)
            def _():
                edge_copy(j, -1).wait_recv()

            image_out[0, part] = raw_out[part] - 0.25 * (raw_near[part] + raw_far[part])

        index_copy(-1).wait_send()
        part_copy(-1).wait_send()
        for j in chunks:
            near_copy(j, -1).wait_send()

        @pl.when(down)
        def _():
            omega_copy().wait_send()
            field_copy(0).wait_send()
            field_copy(1).wait_send()

        @pl.when(jnp.logical_and(down, straight))
        def _():
            pass_copy(raw_out, 1).wait_send()

    @pl.when(even)
    def _():
        for load in loads:
            load.wait()
        mean_own = look_up(0)
        means[0] = jnp.broadcast_to(mean_own, (8, 128))
        pl.semaphore_wait(barrier, 1 + jnp.where(down, 1, 0) + jnp.where(up, 2, 0))

        @pl.when(up)
        def _():
            mean_copy().start()

        @pl.when(down)
        def _():
            omega_copy().start()

        index_copy(1).start()
        phase = phases(omega_of(0), mean_own)
        screen = screens(omega_of(0), 0, mean_own)
        step(own, work, (0, 1), phase, screen)
        first[...] = product(work)
        index_copy(-1).wait_recv()
        mean_next = look_up(1)
        phase = phases(omega_of(0), mean_next)
        screen = screens(omega_of(0), 1, mean_next)
        step(work, own, (0, 1), phase, screen)
        part_out[...] = product(own)
        part_copy(1).start()

        @pl.when(down)
        def _():
            mean_copy().wait_recv()
            phase = phases(omega_of(0), means[1, :1, :1])
            made[0, 0], made[0, 1] = spectral(own, (0,), phase)[0]
            field_copy(0).start()
            made[1, 0], made[1, 1] = spectral(own, (1,), phase)[0]
            for j in chunks:
                tile_copy(j).start()

        @pl.when(up)
        def _():
            omega_copy().wait_recv()

        turns[0], turns[1] = screens(omega_of(1), 0, means[0, :1, :1])
        part_copy(-1).wait_recv()
        first[...] = first[...] + part_in[...]

        @pl.when(up)
        def _():
            field_copy(0).wait_recv()

        for j in chunks:
            part = part_of(j)
            if j == 1:
                for i in chunks:
                    near_copy(i, -1).wait_recv()

                @pl.when(jnp.logical_and(down, jnp.logical_not(straight)))
                def _():
                    field_copy(0).wait_send()
                    tile_copy(0).wait_send()
                    pass_copy(raw_near, 2).start()

            @pl.when(up)
            def _():
                tile_copy(j).wait_recv()

            screen = turns[0, part], turns[1, part]
            s_re, s_im = turned(0, got[0, 0, part], got[0, 1, part], screen)
            r_re, r_im = turned(1, got[1, 0, part], got[1, 1, part], screen)
            raw_out[part] = first[part] + s_re * r_re + s_im * r_im

            @pl.when(up)
            def _():
                edge_copy(j, -1).start()

            near_copy(j, 1).start()
            fields_out[0, 0, 0, part], fields_out[0, 0, 1, part] = s_re, s_im
            fields_out[0, 1, 0, part], fields_out[0, 1, 1, part] = r_re, r_im

        @pl.when(up)
        def _():
            pass_copy(raw_near, 2).wait_recv()

        image_out[0] = raw_out[...] - 0.25 * (raw_near[...] + raw_far[...])

        index_copy(1).wait_send()
        part_copy(1).wait_send()
        for j in chunks:
            near_copy(j, 1).wait_send()

        @pl.when(down)
        def _():
            omega_copy().wait_send()
            for j in range(1, CHUNKS):
                tile_copy(j).wait_send()

        @pl.when(jnp.logical_and(down, straight))
        def _():
            field_copy(0).wait_send()
            tile_copy(0).wait_send()

        @pl.when(jnp.logical_and(down, jnp.logical_not(straight)))
        def _():
            pass_copy(raw_near, 2).wait_send()

        @pl.when(up)
        def _():
            mean_copy().wait_send()
            for j in chunks:
                edge_copy(j, -1).wait_send()


def store(image, fields, image_out, fields_out, sems):
    copies = [
        pltpu.make_async_copy(fields, fields_out, sems.at[0]),
        pltpu.make_async_copy(image, image_out, sems.at[1]),
    ]
    for copy in copies:
        copy.start()
    for copy in copies:
        copy.wait()


def body(fields, freq_index, slowness_index, slowness_table):
    nx, ny = slowness_index.shape[1:]
    count = lax.axis_size("slab")
    assert slowness_index.shape[0] == 1 and count % 2 == 0
    half = ny // 2
    xs, ys, tw = dft_table(nx), dft_table(half), twiddle_table(ny)
    any_spec = pl.BlockSpec(memory_space=pl.ANY)
    vmem_spec = pl.BlockSpec(memory_space=pltpu.VMEM)
    plane = (nx, ny)
    dma = pltpu.SemaphoreType.DMA
    image, moved = pl.pallas_call(
        functools.partial(kernel, count),
        out_shape=(pltpu.VMEM((1, nx, ny), F32), pltpu.VMEM(fields.shape, F32)),
        in_specs=[
            any_spec, pl.BlockSpec(memory_space=pltpu.SMEM), any_spec, any_spec,
            any_spec, any_spec, any_spec,
        ],
        out_specs=(vmem_spec, vmem_spec),
        scratch_shapes=[
            pltpu.VMEM((2, 2) + plane, F32),
            pltpu.VMEM((2, 2) + plane, F32),
            pltpu.VMEM((2, 2) + plane, F32),
            pltpu.VMEM((2, 2) + plane, F32),
            pltpu.VMEM((2,) + plane, jnp.int32),
            pltpu.VMEM((2,) + plane, F32),
            pltpu.VMEM(slowness_table.shape, F32),
            pltpu.VMEM(xs.shape, BF16),
            pltpu.VMEM(ys.shape, BF16),
            pltpu.VMEM(tw.shape, F32),
            pltpu.VMEM((2 * nx, half), F32),
            pltpu.VMEM((2, 8, 128), F32),
            pltpu.VMEM((2, 8, 128), F32),
            pltpu.VMEM((2,) + plane, F32),
            pltpu.VMEM(plane, F32),
            pltpu.VMEM(plane, F32),
            pltpu.VMEM(plane, F32),
            pltpu.VMEM(plane, F32),
            pltpu.VMEM(plane, F32),
            pltpu.VMEM(plane, F32),
            dma((7,)),
            dma((5,)),
            dma((5,)),
            dma((CHUNKS,)),
            dma((CHUNKS,)),
            dma((2,)),
            dma((2,)),
            dma((CHUNKS,)),
            dma((CHUNKS,)),
            dma((CHUNKS,)),
            dma((CHUNKS,)),
        ],
        compiler_params=pltpu.CompilerParams(collective_id=0, has_side_effects=True),
        name="slabs",
    )(
        fields, freq_index, slowness_index, slowness_table,
        jnp.asarray(xs), jnp.asarray(ys), jnp.asarray(tw),
    )
    return pl.pallas_call(
        store,
        out_shape=(
            jax.ShapeDtypeStruct((1, nx, ny), F32),
            jax.ShapeDtypeStruct(fields.shape, F32),
        ),
        in_specs=[vmem_spec, vmem_spec],
        out_specs=(any_spec, any_spec),
        scratch_shapes=[dma((2,))],
        name="store",
    )(
        pltpu.with_memory_space_constraint(image, pltpu.VMEM),
        pltpu.with_memory_space_constraint(moved, pltpu.VMEM),
    )


def solution(mesh):
    return jax.shard_map(
        body,
        mesh=mesh,
        in_specs=(
            P(("shots", "slab"), None, None, None, None),
            P(("shots", "slab")),
            P("slab", None, None),
            P(),
        ),
        out_specs=(P(("shots", "slab"), None, None), P(("shots", "slab"), None, None, None, None)),
        check_vma=False,
    )
```

```python
import functools
import math

import jax
import jax.numpy as jnp
import numpy as np
from jax import lax
from jax.experimental import pallas as pl
from jax.experimental.pallas import tpu as pltpu
from jax.sharding import PartitionSpec as P

NFREQ = 512
SHARES = (3, 2, 2, 1)
CHUNKS = len(SHARES)

F32 = jnp.float32
BF16 = jnp.bfloat16
PI_HI = 3.140625
PI_LO = math.pi - 3.140625


def dft_table(n):
    turn = np.outer(np.arange(n), np.arange(n)) % n * (2.0 * np.pi / n)
    mats = [np.cos(turn), np.sin(turn), -np.sin(turn)]
    high = [mat.astype(BF16) for mat in mats]
    low = [(mat - h.astype(np.float64)).astype(BF16) for mat, h in zip(mats, high)]
    return np.stack(high + low)


def twiddle_table(ny):
    turn = np.arange(ny // 2) * (2.0 * np.pi / ny)
    rows = np.zeros((8, ny // 2), np.float32)
    rows[0], rows[1] = np.cos(turn), np.sin(turn)
    return rows


def split(value):
    high = value.astype(BF16)
    low = (value - high.astype(F32)).astype(BF16)
    return high, low


def cat(values, axis):
    return jnp.concatenate(values, axis=axis)


def block(a, b, c, d):
    return cat([cat([a, b], 1), cat([c, d], 1)], 0)


def dot_data_left(data, high, low):
    d_high, d_low = split(data)
    return jnp.dot(cat([d_high, d_low, d_high], 1), cat([high, high, low], 0), preferred_element_type=F32)


def dot_data_right(high, low, data):
    d_high, d_low = split(data)
    return jnp.dot(cat([high, high, low], 1), cat([d_high, d_low, d_high], 0), preferred_element_type=F32)


def sincos(x):
    turns = jnp.floor(x * (1.0 / math.pi) + 0.5)
    r = (x - turns * PI_HI) - turns * PI_LO
    sign = 1.0 - 2.0 * (turns - 2.0 * jnp.floor(turns * 0.5))
    r2 = r * r
    sin_p = 1.0 / math.factorial(11) * -1.0
    for k, sg in ((9, 1.0), (7, -1.0), (5, 1.0), (3, -1.0)):
        sin_p = sin_p * r2 + sg / math.factorial(k)
    sin_p = r + r * (r2 * sin_p)
    cos_p = 1.0 / math.factorial(12)
    for k, sg in ((10, -1.0), (8, 1.0), (6, -1.0), (4, 1.0), (2, -1.0), (0, 1.0)):
        cos_p = cos_p * r2 + sg / math.factorial(k)
    return sign * sin_p, sign * cos_p


def kernel(
    count, fields, freq, sidx, table, xs_in, ys_in, tw_in, image_out, fields_out,
    own, work, made, got, index, planes, levels, xs, ys, tw, wsq, omegas, means, turns,
    part_out, part_in, raw_out, raw_near, raw_far, first,
    in_sems, far_send, far_recv, tile_send, tile_recv, pair_send, pair_recv,
    near_send, near_recv, edge_send, edge_recv,
):
    me = lax.axis_index("slab")
    nx, ny = index.shape[1:]
    half = ny // 2
    unit = nx // sum(SHARES)
    starts = [unit * sum(SHARES[:j]) for j in range(CHUNKS)]

    def part_of(j):
        return pl.ds(starts[j], unit * SHARES[j])

    odd = lax.rem(me, 2) == 1
    even = jnp.logical_not(odd)
    down = me + 2 < count
    up = me >= 2
    straight = jnp.logical_and(up, lax.rem(me // 2, 2) == 0)

    def to(offset):
        return {"slab": jnp.clip(me + offset, 0, count - 1)}

    loads = [
        pltpu.make_async_copy(fields.at[0, 0], own.at[0], in_sems.at[0]),
        pltpu.make_async_copy(xs_in, xs, in_sems.at[1]),
        pltpu.make_async_copy(table, levels, in_sems.at[2]),
        pltpu.make_async_copy(sidx.at[0], index.at[0], in_sems.at[3]),
        pltpu.make_async_copy(ys_in, ys, in_sems.at[4]),
        pltpu.make_async_copy(tw_in, tw, in_sems.at[5]),
        pltpu.make_async_copy(fields.at[0, 1], own.at[1], in_sems.at[6]),
    ]
    for load in loads:
        load.start()

    barrier = pltpu.get_barrier_semaphore()

    @pl.when(odd)
    def _():
        pl.semaphore_signal(barrier, inc=1, device_id=to(-1))

        @pl.when(down)
        def _():
            pl.semaphore_signal(barrier, inc=1, device_id=to(1))

    @pl.when(even)
    def _():
        pl.semaphore_signal(barrier, inc=1, device_id=to(1))

        @pl.when(up)
        def _():
            pl.semaphore_signal(barrier, inc=1, device_id=to(-1))

    @pl.when(down)
    def _():
        pl.semaphore_signal(barrier, inc=1, device_id=to(2))

    @pl.when(up)
    def _():
        pl.semaphore_signal(barrier, inc=1, device_id=to(-2))

    row = lax.broadcasted_iota(jnp.int32, (nx, half), 0)
    wave_x = jnp.where(row < (nx + 1) // 2, row, row - nx).astype(F32) * (2.0 * math.pi / nx)
    lane = lax.broadcasted_iota(jnp.int32, (1, half), 1)
    for parity in (0, 1):
        k = 2 * lane + parity
        wave_y = jnp.where(k < (ny + 1) // 2, k, k - ny).astype(F32) * (2.0 * math.pi / ny)
        wsq[pl.ds(parity * nx, nx)] = wave_x * wave_x + wave_y * wave_y

    omegas[0] = jnp.full((8, 128), 1.0 + freq[0].astype(F32) / NFREQ, F32)

    @pl.when(jnp.logical_not(up))
    def _():
        got[...] = jnp.zeros(got.shape, F32)
        omegas[1] = jnp.zeros((8, 128), F32)

    @pl.when(jnp.logical_not(jnp.logical_or(odd & down, even & up)))
    def _():
        raw_far[...] = jnp.zeros((nx, ny), F32)

    def look_up(slot):
        pieces = [
            jnp.broadcast_to(levels[pl.ds(j * 128, 128)].reshape(1, 128), (nx, 128))
            for j in range(levels.shape[0] // 128)
        ]
        for h in range(ny // 128):
            cols = pl.ds(h * 128, 128)
            idx = index[slot, :, cols]
            inner = idx & 127
            value = jnp.take_along_axis(pieces[0], inner, axis=1, mode="promise_in_bounds")
            for j in range(1, len(pieces)):
                other = jnp.take_along_axis(pieces[j], inner, axis=1, mode="promise_in_bounds")
                value = jnp.where(idx >= j * 128, other, value)
            planes[slot, :, cols] = value
        columns = jnp.sum(planes[slot], axis=0, keepdims=True)
        return jnp.sum(columns, axis=1, keepdims=True) * (1.0 / (nx * ny))

    def phases(omega, mean_slow):
        q = (omega * mean_slow) ** 2 - wsq[...]
        root = jnp.sqrt(jnp.abs(q))
        sin_v, cos_v = sincos(root)
        moving = q > 0.0
        scale = 1.0 / (nx * ny)
        cos_p = jnp.where(moving, cos_v, jnp.exp(-root)) * scale
        sin_p = jnp.where(moving, sin_v, 0.0) * scale
        return cos_p, sin_p

    def screens(omega, slot, mean_slow):
        return sincos(omega * (planes[slot] - mean_slow))

    def spectral(source, which, phase):
        x_c, x_s, x_n = ((xs[i], xs[i + 3]) for i in range(3))
        y_c, y_s, y_n = ((ys[i], ys[i + 3]) for i in range(3))
        x_fwd = [block(x_c[i], x_s[i], x_n[i], x_c[i]) for i in (0, 1)]
        x_inv = [block(x_c[i], x_n[i], x_s[i], x_c[i]) for i in (0, 1)]
        y_fwd = [block(y_c[i], y_n[i], y_s[i], y_c[i]) for i in (0, 1)]
        y_inv = [block(y_c[i], y_s[i], y_n[i], y_c[i]) for i in (0, 1)]
        tw_c, tw_s = tw[:1], tw[1:2]
        cos_p, sin_p = phase
        mixed = []
        for f in which:
            spec = dot_data_right(*x_fwd, cat([source[f, 0], source[f, 1]], 0))
            left, right = spec[:, :half], spec[:, half:]
            plus, minus = left + right, left - right
            m_re, m_im = minus[:nx], minus[nx:]
            mixed.append(cat([
                cat([plus[:nx], plus[nx:]], 1),
                cat([m_re * tw_c + m_im * tw_s, m_im * tw_c - m_re * tw_s], 1),
            ], 0))
        spectrum = dot_data_left(cat(mixed, 0), *y_fwd)
        shifted = []
        for at, f in enumerate(which):
            v = spectrum[at * 2 * nx:(at + 1) * 2 * nx]
            v_re, v_im = v[:, :half], v[:, half:]
            if f == 0:
                shifted.append(cat([v_re * cos_p - v_im * sin_p, v_re * sin_p + v_im * cos_p], 1))
            else:
                shifted.append(cat([v_re * cos_p + v_im * sin_p, v_im * cos_p - v_re * sin_p], 1))
        back = dot_data_left(cat(shifted, 0), *y_inv)
        out = []
        for at, f in enumerate(which):
            b = back[at * 2 * nx:(at + 1) * 2 * nx]
            e_re, e_im = b[:nx, :half], b[:nx, half:]
            t_re, t_im = b[nx:, :half], b[nx:, half:]
            o_re, o_im = t_re * tw_c - t_im * tw_s, t_im * tw_c + t_re * tw_s
            moved = dot_data_right(*x_inv, cat([
                cat([e_re + o_re, e_re - o_re], 1), cat([e_im + o_im, e_im - o_im], 1),
            ], 0))
            out.append((moved[:nx], moved[nx:]))
        return out

    def turned(f, b_re, b_im, screen):
        s_sin, s_cos = screen
        if f == 0:
            return b_re * s_cos - b_im * s_sin, b_re * s_sin + b_im * s_cos
        return b_re * s_cos + b_im * s_sin, b_im * s_cos - b_re * s_sin

    def step(source, target, which, phase, screen):
        for f, (b_re, b_im) in zip(which, spectral(source, which, phase)):
            target[f, 0], target[f, 1] = turned(f, b_re, b_im, screen)

    def product(ref):
        return ref[0, 0] * ref[1, 0] + ref[0, 1] * ref[1, 1]

    def omega_of(slot):
        return omegas[slot, :1, :1]

    def remote(src, dst, send, recv, offset):
        return pltpu.make_async_remote_copy(
            src_ref=src, dst_ref=dst, send_sem=send, recv_sem=recv, device_id=to(offset)
        )

    def field_copy(f):
        return remote(made.at[f], got.at[f], far_send.at[f], far_recv.at[f], 2)

    def omega_copy():
        return remote(omegas.at[0], omegas.at[1], far_send.at[2], far_recv.at[2], 2)

    def mean_copy():
        return remote(means.at[0], means.at[1], far_send.at[3], far_recv.at[3], -2)

    def tile_copy(j):
        part = part_of(j)
        return remote(
            made.at[1, :, part], got.at[1, :, part], tile_send.at[j], tile_recv.at[j], 2
        )

    def index_copy(offset):
        return remote(sidx.at[0], index.at[1], pair_send.at[0], pair_recv.at[0], offset)

    def part_copy(offset):
        return remote(part_out, part_in, pair_send.at[1], pair_recv.at[1], offset)

    def near_copy(j, offset):
        part = part_of(j)
        return remote(raw_out.at[part], raw_near.at[part], near_send.at[j], near_recv.at[j], offset)

    def edge_copy(j, offset):
        part = part_of(j)
        return remote(raw_out.at[part], raw_far.at[part], edge_send.at[j], edge_recv.at[j], offset)

    def pass_copy(source, offset):
        return remote(source, raw_far, far_send.at[4], far_recv.at[4], offset)

    chunks = range(CHUNKS)

    @pl.when(odd)
    def _():
        for load in loads[:6]:
            load.wait()
        mean_own = look_up(0)
        phase = phases(omega_of(0), mean_own)
        screen_own = screens(omega_of(0), 0, mean_own)
        step(own, made, (0,), phase, screen_own)
        pl.semaphore_wait(barrier, 1 + jnp.where(down, 2, 0) + jnp.where(up, 1, 0))

        @pl.when(down)
        def _():
            omega_copy().start()
            field_copy(0).start()

        index_copy(-1).start()
        loads[6].wait()
        step(own, made, (1,), phase, screen_own)

        @pl.when(down)
        def _():
            field_copy(1).start()

        first[...] = product(made)
        index_copy(1).wait_recv()

        @pl.when(up)
        def _():
            omega_copy().wait_recv()

        mean_low = look_up(1)
        phase_0 = phases(omega_of(1), mean_low)
        screen_0 = screens(omega_of(1), 1, mean_low)
        phase_1 = phases(omega_of(1), mean_own)
        screen_1 = screens(omega_of(1), 0, mean_own)

        @pl.when(up)
        def _():
            field_copy(0).wait_recv()

        step(got, work, (0,), phase_0, screen_0)
        step(work, fields_out.at[0], (0,), phase_1, screen_1)

        @pl.when(up)
        def _():
            field_copy(1).wait_recv()

        step(got, work, (1,), phase_0, screen_0)
        part_out[...] = product(work)
        part_copy(-1).start()
        step(work, fields_out.at[0], (1,), phase_1, screen_1)
        part_copy(1).wait_recv()
        raw_out[...] = first[...] + part_in[...] + product(fields_out.at[0])
        @pl.when(jnp.logical_and(down, straight))
        def _():
            pass_copy(raw_out, 1).start()

        for j in chunks:
            near_copy(j, -1).start()

        for j in chunks:
            part = part_of(j)
            near_copy(j, 1).wait_recv()

            @pl.when(down)
            def _():
                edge_copy(j, -1).wait_recv()

            image_out[0, part] = raw_out[part] - 0.25 * (raw_near[part] + raw_far[part])

        index_copy(-1).wait_send()
        part_copy(-1).wait_send()
        for j in chunks:
            near_copy(j, -1).wait_send()

        @pl.when(down)
        def _():
            omega_copy().wait_send()
            field_copy(0).wait_send()
            field_copy(1).wait_send()

        @pl.when(jnp.logical_and(down, straight))
        def _():
            pass_copy(raw_out, 1).wait_send()

    @pl.when(even)
    def _():
        for load in loads:
            load.wait()
        mean_own = look_up(0)
        means[0] = jnp.broadcast_to(mean_own, (8, 128))
        pl.semaphore_wait(barrier, 1 + jnp.where(down, 1, 0) + jnp.where(up, 2, 0))

        @pl.when(up)
        def _():
            mean_copy().start()

        @pl.when(down)
        def _():
            omega_copy().start()

        index_copy(1).start()
        phase = phases(omega_of(0), mean_own)
        screen = screens(omega_of(0), 0, mean_own)
        step(own, work, (0, 1), phase, screen)
        first[...] = product(work)
        index_copy(-1).wait_recv()
        mean_next = look_up(1)
        phase = phases(omega_of(0), mean_next)
        screen = screens(omega_of(0), 1, mean_next)
        step(work, own, (0, 1), phase, screen)
        part_out[...] = product(own)
        part_copy(1).start()

        @pl.when(down)
        def _():
            mean_copy().wait_recv()
            phase = phases(omega_of(0), means[1, :1, :1])
            made[0, 0], made[0, 1] = spectral(own, (0,), phase)[0]
            field_copy(0).start()
            made[1, 0], made[1, 1] = spectral(own, (1,), phase)[0]
            for j in chunks:
                tile_copy(j).start()

        @pl.when(up)
        def _():
            omega_copy().wait_recv()

        turns[0], turns[1] = screens(omega_of(1), 0, means[0, :1, :1])
        part_copy(-1).wait_recv()
        first[...] = first[...] + part_in[...]

        @pl.when(up)
        def _():
            field_copy(0).wait_recv()

        for j in chunks:
            part = part_of(j)
            if j == 2:
                for i in chunks:
                    near_copy(i, -1).wait_recv()

                @pl.when(jnp.logical_and(down, jnp.logical_not(straight)))
                def _():
                    field_copy(0).wait_send()
                    tile_copy(0).wait_send()
                    tile_copy(1).wait_send()
                    pass_copy(raw_near, 2).start()

            @pl.when(up)
            def _():
                tile_copy(j).wait_recv()

            screen = turns[0, part], turns[1, part]
            s_re, s_im = turned(0, got[0, 0, part], got[0, 1, part], screen)
            r_re, r_im = turned(1, got[1, 0, part], got[1, 1, part], screen)
            raw_out[part] = first[part] + s_re * r_re + s_im * r_im

            @pl.when(up)
            def _():
                edge_copy(j, -1).start()

            if j == CHUNKS - 1:
                for i in chunks:
                    near_copy(i, 1).start()

            fields_out[0, 0, 0, part], fields_out[0, 0, 1, part] = s_re, s_im
            fields_out[0, 1, 0, part], fields_out[0, 1, 1, part] = r_re, r_im

        @pl.when(up)
        def _():
            pass_copy(raw_near, 2).wait_recv()

        image_out[0] = raw_out[...] - 0.25 * (raw_near[...] + raw_far[...])

        index_copy(1).wait_send()
        part_copy(1).wait_send()
        for j in chunks:
            near_copy(j, 1).wait_send()

        @pl.when(down)
        def _():
            omega_copy().wait_send()
            for j in range(2, CHUNKS):
                tile_copy(j).wait_send()

        @pl.when(jnp.logical_and(down, straight))
        def _():
            field_copy(0).wait_send()
            tile_copy(0).wait_send()
            tile_copy(1).wait_send()

        @pl.when(jnp.logical_and(down, jnp.logical_not(straight)))
        def _():
            pass_copy(raw_near, 2).wait_send()

        @pl.when(up)
        def _():
            mean_copy().wait_send()
            for j in chunks:
                edge_copy(j, -1).wait_send()


def store(image, fields, image_out, fields_out, sems):
    copies = [
        pltpu.make_async_copy(fields, fields_out, sems.at[0]),
        pltpu.make_async_copy(image, image_out, sems.at[1]),
    ]
    for copy in copies:
        copy.start()
    for copy in copies:
        copy.wait()


def body(fields, freq_index, slowness_index, slowness_table):
    nx, ny = slowness_index.shape[1:]
    count = lax.axis_size("slab")
    assert slowness_index.shape[0] == 1 and count % 2 == 0
    half = ny // 2
    xs, ys, tw = dft_table(nx), dft_table(half), twiddle_table(ny)
    any_spec = pl.BlockSpec(memory_space=pl.ANY)
    vmem_spec = pl.BlockSpec(memory_space=pltpu.VMEM)
    plane = (nx, ny)
    dma = pltpu.SemaphoreType.DMA
    image, moved = pl.pallas_call(
        functools.partial(kernel, count),
        out_shape=(pltpu.VMEM((1, nx, ny), F32), pltpu.VMEM(fields.shape, F32)),
        in_specs=[
            any_spec, pl.BlockSpec(memory_space=pltpu.SMEM), any_spec, any_spec,
            any_spec, any_spec, any_spec,
        ],
        out_specs=(vmem_spec, vmem_spec),
        scratch_shapes=[
            pltpu.VMEM((2, 2) + plane, F32),
            pltpu.VMEM((2, 2) + plane, F32),
            pltpu.VMEM((2, 2) + plane, F32),
            pltpu.VMEM((2, 2) + plane, F32),
            pltpu.VMEM((2,) + plane, jnp.int32),
            pltpu.VMEM((2,) + plane, F32),
            pltpu.VMEM(slowness_table.shape, F32),
            pltpu.VMEM(xs.shape, BF16),
            pltpu.VMEM(ys.shape, BF16),
            pltpu.VMEM(tw.shape, F32),
            pltpu.VMEM((2 * nx, half), F32),
            pltpu.VMEM((2, 8, 128), F32),
            pltpu.VMEM((2, 8, 128), F32),
            pltpu.VMEM((2,) + plane, F32),
            pltpu.VMEM(plane, F32),
            pltpu.VMEM(plane, F32),
            pltpu.VMEM(plane, F32),
            pltpu.VMEM(plane, F32),
            pltpu.VMEM(plane, F32),
            pltpu.VMEM(plane, F32),
            dma((7,)),
            dma((5,)),
            dma((5,)),
            dma((CHUNKS,)),
            dma((CHUNKS,)),
            dma((2,)),
            dma((2,)),
            dma((CHUNKS,)),
            dma((CHUNKS,)),
            dma((CHUNKS,)),
            dma((CHUNKS,)),
        ],
        compiler_params=pltpu.CompilerParams(collective_id=0, has_side_effects=True),
        name="slabs",
    )(
        fields, freq_index, slowness_index, slowness_table,
        jnp.asarray(xs), jnp.asarray(ys), jnp.asarray(tw),
    )
    return pl.pallas_call(
        store,
        out_shape=(
            jax.ShapeDtypeStruct((1, nx, ny), F32),
            jax.ShapeDtypeStruct(fields.shape, F32),
        ),
        in_specs=[vmem_spec, vmem_spec],
        out_specs=(any_spec, any_spec),
        scratch_shapes=[dma((2,))],
        name="store",
    )(
        pltpu.with_memory_space_constraint(image, pltpu.VMEM),
        pltpu.with_memory_space_constraint(moved, pltpu.VMEM),
    )


def solution(mesh):
    return jax.shard_map(
        body,
        mesh=mesh,
        in_specs=(
            P(("shots", "slab"), None, None, None, None),
            P(("shots", "slab")),
            P("slab", None, None),
            P(),
        ),
        out_specs=(P(("shots", "slab"), None, None), P(("shots", "slab"), None, None, None, None)),
        check_vma=False,
    )
```

```python
import functools
import math

import jax
import jax.numpy as jnp
import numpy as np
from jax import lax
from jax.experimental import pallas as pl
from jax.experimental.pallas import tpu as pltpu
from jax.sharding import PartitionSpec as P

NFREQ = 512
SHARES = (3, 2, 2, 1)
CHUNKS = len(SHARES)

F32 = jnp.float32
BF16 = jnp.bfloat16
PI_HI = 3.140625
PI_LO = math.pi - 3.140625


def dft_table(n):
    turn = np.outer(np.arange(n), np.arange(n)) % n * (2.0 * np.pi / n)
    mats = [np.cos(turn), np.sin(turn), -np.sin(turn)]
    high = [mat.astype(BF16) for mat in mats]
    low = [(mat - h.astype(np.float64)).astype(BF16) for mat, h in zip(mats, high)]
    return np.stack(high + low)


def twiddle_table(ny):
    turn = np.arange(ny // 2) * (2.0 * np.pi / ny)
    rows = np.zeros((8, ny // 2), np.float32)
    rows[0], rows[1] = np.cos(turn), np.sin(turn)
    return rows


def split(value):
    high = value.astype(BF16)
    low = (value - high.astype(F32)).astype(BF16)
    return high, low


def cat(values, axis):
    return jnp.concatenate(values, axis=axis)


def block(a, b, c, d):
    return cat([cat([a, b], 1), cat([c, d], 1)], 0)


def dot_data_left(data, high, low):
    d_high, d_low = split(data)
    return jnp.dot(cat([d_high, d_low, d_high], 1), cat([high, high, low], 0), preferred_element_type=F32)


def dot_data_right(high, low, data):
    d_high, d_low = split(data)
    return jnp.dot(cat([high, high, low], 1), cat([d_high, d_low, d_high], 0), preferred_element_type=F32)


def sincos(x):
    turns = jnp.floor(x * (1.0 / math.pi) + 0.5)
    r = (x - turns * PI_HI) - turns * PI_LO
    sign = 1.0 - 2.0 * (turns - 2.0 * jnp.floor(turns * 0.5))
    r2 = r * r
    sin_p = 1.0 / math.factorial(11) * -1.0
    for k, sg in ((9, 1.0), (7, -1.0), (5, 1.0), (3, -1.0)):
        sin_p = sin_p * r2 + sg / math.factorial(k)
    sin_p = r + r * (r2 * sin_p)
    cos_p = 1.0 / math.factorial(12)
    for k, sg in ((10, -1.0), (8, 1.0), (6, -1.0), (4, 1.0), (2, -1.0), (0, 1.0)):
        cos_p = cos_p * r2 + sg / math.factorial(k)
    return sign * sin_p, sign * cos_p


def kernel(
    count, fields, freq, sidx, table, xs_in, ys_in, tw_in, image_out, fields_out,
    own, work, made, got, index, planes, levels, xs, ys, tw, wsq, omegas, means, turns,
    part_out, part_in, raw_out, raw_near, raw_far, first,
    in_sems, far_send, far_recv, tile_send, tile_recv, pair_send, pair_recv,
    near_send, near_recv, edge_send, edge_recv,
):
    me = lax.axis_index("slab")
    nx, ny = index.shape[1:]
    half = ny // 2
    unit = nx // sum(SHARES)
    starts = [unit * sum(SHARES[:j]) for j in range(CHUNKS)]

    def part_of(j):
        return pl.ds(starts[j], unit * SHARES[j])

    odd = lax.rem(me, 2) == 1
    even = jnp.logical_not(odd)
    down = me + 2 < count
    up = me >= 2
    straight = jnp.logical_and(up, lax.rem(me // 2, 2) == 0)

    def to(offset):
        return {"slab": jnp.clip(me + offset, 0, count - 1)}

    loads = [
        pltpu.make_async_copy(fields.at[0, 0], own.at[0], in_sems.at[0]),
        pltpu.make_async_copy(xs_in, xs, in_sems.at[1]),
        pltpu.make_async_copy(table, levels, in_sems.at[2]),
        pltpu.make_async_copy(sidx.at[0], index.at[0], in_sems.at[3]),
        pltpu.make_async_copy(ys_in, ys, in_sems.at[4]),
        pltpu.make_async_copy(tw_in, tw, in_sems.at[5]),
        pltpu.make_async_copy(fields.at[0, 1], own.at[1], in_sems.at[6]),
    ]
    for load in loads:
        load.start()

    barrier = pltpu.get_barrier_semaphore()

    @pl.when(odd)
    def _():
        pl.semaphore_signal(barrier, inc=1, device_id=to(-1))

        @pl.when(down)
        def _():
            pl.semaphore_signal(barrier, inc=1, device_id=to(1))

    @pl.when(even)
    def _():
        pl.semaphore_signal(barrier, inc=1, device_id=to(1))

        @pl.when(up)
        def _():
            pl.semaphore_signal(barrier, inc=1, device_id=to(-1))

    @pl.when(down)
    def _():
        pl.semaphore_signal(barrier, inc=1, device_id=to(2))

    @pl.when(up)
    def _():
        pl.semaphore_signal(barrier, inc=1, device_id=to(-2))

    row = lax.broadcasted_iota(jnp.int32, (nx, half), 0)
    wave_x = jnp.where(row < (nx + 1) // 2, row, row - nx).astype(F32) * (2.0 * math.pi / nx)
    lane = lax.broadcasted_iota(jnp.int32, (1, half), 1)
    for parity in (0, 1):
        k = 2 * lane + parity
        wave_y = jnp.where(k < (ny + 1) // 2, k, k - ny).astype(F32) * (2.0 * math.pi / ny)
        wsq[pl.ds(parity * nx, nx)] = wave_x * wave_x + wave_y * wave_y

    omegas[0] = jnp.full((8, 128), 1.0 + freq[0].astype(F32) / NFREQ, F32)

    @pl.when(jnp.logical_not(up))
    def _():
        got[...] = jnp.zeros(got.shape, F32)
        omegas[1] = jnp.zeros((8, 128), F32)

    @pl.when(jnp.logical_not(jnp.logical_or(odd & down, even & up)))
    def _():
        raw_far[...] = jnp.zeros((nx, ny), F32)

    def look_up(slot):
        pieces = [
            jnp.broadcast_to(levels[pl.ds(j * 128, 128)].reshape(1, 128), (nx, 128))
            for j in range(levels.shape[0] // 128)
        ]
        for h in range(ny // 128):
            cols = pl.ds(h * 128, 128)
            idx = index[slot, :, cols]
            inner = idx & 127
            value = jnp.take_along_axis(pieces[0], inner, axis=1, mode="promise_in_bounds")
            for j in range(1, len(pieces)):
                other = jnp.take_along_axis(pieces[j], inner, axis=1, mode="promise_in_bounds")
                value = jnp.where(idx >= j * 128, other, value)
            planes[slot, :, cols] = value
        columns = jnp.sum(planes[slot], axis=0, keepdims=True)
        return jnp.sum(columns, axis=1, keepdims=True) * (1.0 / (nx * ny))

    def phases(omega, mean_slow):
        q = (omega * mean_slow) ** 2 - wsq[...]
        root = jnp.sqrt(jnp.abs(q))
        sin_v, cos_v = sincos(root)
        moving = q > 0.0
        scale = 1.0 / (nx * ny)
        cos_p = jnp.where(moving, cos_v, jnp.exp(-root)) * scale
        sin_p = jnp.where(moving, sin_v, 0.0) * scale
        return cos_p, sin_p

    def screens(omega, slot, mean_slow):
        return sincos(omega * (planes[slot] - mean_slow))

    def spectral(source, which, phase):
        x_c, x_s, x_n = ((xs[i], xs[i + 3]) for i in range(3))
        y_c, y_s, y_n = ((ys[i], ys[i + 3]) for i in range(3))
        x_fwd = [block(x_c[i], x_s[i], x_n[i], x_c[i]) for i in (0, 1)]
        x_inv = [block(x_c[i], x_n[i], x_s[i], x_c[i]) for i in (0, 1)]
        y_fwd = [block(y_c[i], y_n[i], y_s[i], y_c[i]) for i in (0, 1)]
        y_inv = [block(y_c[i], y_s[i], y_n[i], y_c[i]) for i in (0, 1)]
        tw_c, tw_s = tw[:1], tw[1:2]
        cos_p, sin_p = phase
        mixed = []
        for f in which:
            spec = dot_data_right(*x_fwd, cat([source[f, 0], source[f, 1]], 0))
            left, right = spec[:, :half], spec[:, half:]
            plus, minus = left + right, left - right
            m_re, m_im = minus[:nx], minus[nx:]
            mixed.append(cat([
                cat([plus[:nx], plus[nx:]], 1),
                cat([m_re * tw_c + m_im * tw_s, m_im * tw_c - m_re * tw_s], 1),
            ], 0))
        spectrum = dot_data_left(cat(mixed, 0), *y_fwd)
        shifted = []
        for at, f in enumerate(which):
            v = spectrum[at * 2 * nx:(at + 1) * 2 * nx]
            v_re, v_im = v[:, :half], v[:, half:]
            if f == 0:
                shifted.append(cat([v_re * cos_p - v_im * sin_p, v_re * sin_p + v_im * cos_p], 1))
            else:
                shifted.append(cat([v_re * cos_p + v_im * sin_p, v_im * cos_p - v_re * sin_p], 1))
        back = dot_data_left(cat(shifted, 0), *y_inv)
        out = []
        for at, f in enumerate(which):
            b = back[at * 2 * nx:(at + 1) * 2 * nx]
            e_re, e_im = b[:nx, :half], b[:nx, half:]
            t_re, t_im = b[nx:, :half], b[nx:, half:]
            o_re, o_im = t_re * tw_c - t_im * tw_s, t_im * tw_c + t_re * tw_s
            moved = dot_data_right(*x_inv, cat([
                cat([e_re + o_re, e_re - o_re], 1), cat([e_im + o_im, e_im - o_im], 1),
            ], 0))
            out.append((moved[:nx], moved[nx:]))
        return out

    def turned(f, b_re, b_im, screen):
        s_sin, s_cos = screen
        if f == 0:
            return b_re * s_cos - b_im * s_sin, b_re * s_sin + b_im * s_cos
        return b_re * s_cos + b_im * s_sin, b_im * s_cos - b_re * s_sin

    def step(source, target, which, phase, screen):
        for f, (b_re, b_im) in zip(which, spectral(source, which, phase)):
            target[f, 0], target[f, 1] = turned(f, b_re, b_im, screen)

    def product(ref):
        return ref[0, 0] * ref[1, 0] + ref[0, 1] * ref[1, 1]

    def omega_of(slot):
        return omegas[slot, :1, :1]

    def remote(src, dst, send, recv, offset):
        return pltpu.make_async_remote_copy(
            src_ref=src, dst_ref=dst, send_sem=send, recv_sem=recv, device_id=to(offset)
        )

    def field_copy(f):
        return remote(made.at[f], got.at[f], far_send.at[f], far_recv.at[f], 2)

    def omega_copy():
        return remote(omegas.at[0], omegas.at[1], far_send.at[2], far_recv.at[2], 2)

    def mean_copy():
        return remote(means.at[0], means.at[1], far_send.at[3], far_recv.at[3], -2)

    def tile_copy(j):
        part = part_of(j)
        return remote(
            made.at[1, :, part], got.at[1, :, part], tile_send.at[j], tile_recv.at[j], 2
        )

    def index_copy(offset):
        return remote(sidx.at[0], index.at[1], pair_send.at[0], pair_recv.at[0], offset)

    def part_copy(offset):
        return remote(part_out, part_in, pair_send.at[1], pair_recv.at[1], offset)

    def near_copy(j, offset):
        part = part_of(j)
        return remote(raw_out.at[part], raw_near.at[part], near_send.at[j], near_recv.at[j], offset)

    def edge_copy(j, offset):
        part = part_of(j)
        return remote(raw_out.at[part], raw_far.at[part], edge_send.at[j], edge_recv.at[j], offset)

    def pass_copy(source, offset):
        return remote(source, raw_far, far_send.at[4], far_recv.at[4], offset)

    chunks = range(CHUNKS)

    @pl.when(odd)
    def _():
        for load in loads[:6]:
            load.wait()
        mean_own = look_up(0)
        phase = phases(omega_of(0), mean_own)
        screen_own = screens(omega_of(0), 0, mean_own)
        step(own, made, (0,), phase, screen_own)
        pl.semaphore_wait(barrier, 1 + jnp.where(down, 2, 0) + jnp.where(up, 1, 0))

        @pl.when(down)
        def _():
            omega_copy().start()
            field_copy(0).start()

        index_copy(-1).start()
        loads[6].wait()
        step(own, made, (1,), phase, screen_own)

        @pl.when(down)
        def _():
            field_copy(1).start()

        first[...] = product(made)
        index_copy(1).wait_recv()

        @pl.when(up)
        def _():
            omega_copy().wait_recv()

        mean_low = look_up(1)
        phase_0 = phases(omega_of(1), mean_low)
        screen_0 = screens(omega_of(1), 1, mean_low)
        phase_1 = phases(omega_of(1), mean_own)
        screen_1 = screens(omega_of(1), 0, mean_own)

        @pl.when(up)
        def _():
            field_copy(0).wait_recv()

        step(got, work, (0,), phase_0, screen_0)
        step(work, fields_out.at[0], (0,), phase_1, screen_1)

        @pl.when(up)
        def _():
            field_copy(1).wait_recv()

        step(got, work, (1,), phase_0, screen_0)
        part_out[...] = product(work)
        part_copy(-1).start()
        step(work, fields_out.at[0], (1,), phase_1, screen_1)
        part_copy(1).wait_recv()
        raw_out[...] = first[...] + part_in[...] + product(fields_out.at[0])
        @pl.when(jnp.logical_and(down, straight))
        def _():
            pass_copy(raw_out, 1).start()

        for j in chunks:
            near_copy(j, -1).start()

        for j in chunks:
            part = part_of(j)
            near_copy(j, 1).wait_recv()

            @pl.when(down)
            def _():
                edge_copy(j, -1).wait_recv()

            image_out[0, part] = raw_out[part] - 0.25 * (raw_near[part] + raw_far[part])

        index_copy(-1).wait_send()
        part_copy(-1).wait_send()
        for j in chunks:
            near_copy(j, -1).wait_send()

        @pl.when(down)
        def _():
            omega_copy().wait_send()
            field_copy(0).wait_send()
            field_copy(1).wait_send()

        @pl.when(jnp.logical_and(down, straight))
        def _():
            pass_copy(raw_out, 1).wait_send()

    @pl.when(even)
    def _():
        for load in loads:
            load.wait()
        mean_own = look_up(0)
        means[0] = jnp.broadcast_to(mean_own, (8, 128))
        pl.semaphore_wait(barrier, 1 + jnp.where(down, 1, 0) + jnp.where(up, 2, 0))

        @pl.when(up)
        def _():
            mean_copy().start()

        @pl.when(down)
        def _():
            omega_copy().start()

        index_copy(1).start()
        phase = phases(omega_of(0), mean_own)
        screen = screens(omega_of(0), 0, mean_own)
        step(own, work, (0, 1), phase, screen)
        first[...] = product(work)
        index_copy(-1).wait_recv()
        mean_next = look_up(1)
        phase = phases(omega_of(0), mean_next)
        screen = screens(omega_of(0), 1, mean_next)
        step(work, own, (0, 1), phase, screen)
        part_out[...] = product(own)
        part_copy(1).start()

        @pl.when(down)
        def _():
            mean_copy().wait_recv()
            phase = phases(omega_of(0), means[1, :1, :1])
            made[0, 0], made[0, 1] = spectral(own, (0,), phase)[0]
            field_copy(0).start()
            made[1, 0], made[1, 1] = spectral(own, (1,), phase)[0]
            for j in chunks:
                tile_copy(j).start()

        @pl.when(up)
        def _():
            omega_copy().wait_recv()

        turns[0], turns[1] = screens(omega_of(1), 0, means[0, :1, :1])
        part_copy(-1).wait_recv()
        first[...] = first[...] + part_in[...]

        @pl.when(up)
        def _():
            field_copy(0).wait_recv()

        for j in chunks:
            part = part_of(j)
            if j == 1:
                for i in chunks:
                    near_copy(i, -1).wait_recv()

                @pl.when(jnp.logical_and(down, jnp.logical_not(straight)))
                def _():
                    field_copy(0).wait_send()
                    tile_copy(0).wait_send()
                    pass_copy(raw_near, 2).start()

            @pl.when(up)
            def _():
                tile_copy(j).wait_recv()

            screen = turns[0, part], turns[1, part]
            s_re, s_im = turned(0, got[0, 0, part], got[0, 1, part], screen)
            r_re, r_im = turned(1, got[1, 0, part], got[1, 1, part], screen)
            raw_out[part] = first[part] + s_re * r_re + s_im * r_im

            @pl.when(up)
            def _():
                edge_copy(j, -1).start()

            if j == CHUNKS - 1:
                for i in chunks:
                    near_copy(i, 1).start()

            fields_out[0, 0, 0, part], fields_out[0, 0, 1, part] = s_re, s_im
            fields_out[0, 1, 0, part], fields_out[0, 1, 1, part] = r_re, r_im

        @pl.when(up)
        def _():
            pass_copy(raw_near, 2).wait_recv()

        image_out[0] = raw_out[...] - 0.25 * (raw_near[...] + raw_far[...])

        index_copy(1).wait_send()
        part_copy(1).wait_send()
        for j in chunks:
            near_copy(j, 1).wait_send()

        @pl.when(down)
        def _():
            omega_copy().wait_send()
            for j in range(1, CHUNKS):
                tile_copy(j).wait_send()

        @pl.when(jnp.logical_and(down, straight))
        def _():
            field_copy(0).wait_send()
            tile_copy(0).wait_send()

        @pl.when(jnp.logical_and(down, jnp.logical_not(straight)))
        def _():
            pass_copy(raw_near, 2).wait_send()

        @pl.when(up)
        def _():
            mean_copy().wait_send()
            for j in chunks:
                edge_copy(j, -1).wait_send()


def store(image, fields, image_out, fields_out, sems):
    copies = [
        pltpu.make_async_copy(fields, fields_out, sems.at[0]),
        pltpu.make_async_copy(image, image_out, sems.at[1]),
    ]
    for copy in copies:
        copy.start()
    for copy in copies:
        copy.wait()


def body(fields, freq_index, slowness_index, slowness_table):
    nx, ny = slowness_index.shape[1:]
    count = lax.axis_size("slab")
    assert slowness_index.shape[0] == 1 and count % 2 == 0
    half = ny // 2
    xs, ys, tw = dft_table(nx), dft_table(half), twiddle_table(ny)
    any_spec = pl.BlockSpec(memory_space=pl.ANY)
    vmem_spec = pl.BlockSpec(memory_space=pltpu.VMEM)
    plane = (nx, ny)
    dma = pltpu.SemaphoreType.DMA
    image, moved = pl.pallas_call(
        functools.partial(kernel, count),
        out_shape=(pltpu.VMEM((1, nx, ny), F32), pltpu.VMEM(fields.shape, F32)),
        in_specs=[
            any_spec, pl.BlockSpec(memory_space=pltpu.SMEM), any_spec, any_spec,
            any_spec, any_spec, any_spec,
        ],
        out_specs=(vmem_spec, vmem_spec),
        scratch_shapes=[
            pltpu.VMEM((2, 2) + plane, F32),
            pltpu.VMEM((2, 2) + plane, F32),
            pltpu.VMEM((2, 2) + plane, F32),
            pltpu.VMEM((2, 2) + plane, F32),
            pltpu.VMEM((2,) + plane, jnp.int32),
            pltpu.VMEM((2,) + plane, F32),
            pltpu.VMEM(slowness_table.shape, F32),
            pltpu.VMEM(xs.shape, BF16),
            pltpu.VMEM(ys.shape, BF16),
            pltpu.VMEM(tw.shape, F32),
            pltpu.VMEM((2 * nx, half), F32),
            pltpu.VMEM((2, 8, 128), F32),
            pltpu.VMEM((2, 8, 128), F32),
            pltpu.VMEM((2,) + plane, F32),
            pltpu.VMEM(plane, F32),
            pltpu.VMEM(plane, F32),
            pltpu.VMEM(plane, F32),
            pltpu.VMEM(plane, F32),
            pltpu.VMEM(plane, F32),
            pltpu.VMEM(plane, F32),
            dma((7,)),
            dma((5,)),
            dma((5,)),
            dma((CHUNKS,)),
            dma((CHUNKS,)),
            dma((2,)),
            dma((2,)),
            dma((CHUNKS,)),
            dma((CHUNKS,)),
            dma((CHUNKS,)),
            dma((CHUNKS,)),
        ],
        compiler_params=pltpu.CompilerParams(collective_id=0, has_side_effects=True),
        name="slabs",
    )(
        fields, freq_index, slowness_index, slowness_table,
        jnp.asarray(xs), jnp.asarray(ys), jnp.asarray(tw),
    )
    return pl.pallas_call(
        store,
        out_shape=(
            jax.ShapeDtypeStruct((1, nx, ny), F32),
            jax.ShapeDtypeStruct(fields.shape, F32),
        ),
        in_specs=[vmem_spec, vmem_spec],
        out_specs=(any_spec, any_spec),
        scratch_shapes=[dma((2,))],
        name="store",
    )(
        pltpu.with_memory_space_constraint(image, pltpu.VMEM),
        pltpu.with_memory_space_constraint(moved, pltpu.VMEM),
    )


def solution(mesh):
    return jax.shard_map(
        body,
        mesh=mesh,
        in_specs=(
            P(("shots", "slab"), None, None, None, None),
            P(("shots", "slab")),
            P("slab", None, None),
            P(),
        ),
        out_specs=(P(("shots", "slab"), None, None), P(("shots", "slab"), None, None, None, None)),
        check_vma=False,
    )
```

```python
import functools
import math

import jax
import jax.numpy as jnp
import numpy as np
from jax import lax
from jax.experimental import pallas as pl
from jax.experimental.pallas import tpu as pltpu
from jax.sharding import PartitionSpec as P

NFREQ = 512
SHARES = (3, 2, 2, 1)
CHUNKS = len(SHARES)

F32 = jnp.float32
BF16 = jnp.bfloat16
PI_HI = 3.140625
PI_LO = math.pi - 3.140625


def dft_table(n):
    turn = np.outer(np.arange(n), np.arange(n)) % n * (2.0 * np.pi / n)
    mats = [np.cos(turn), np.sin(turn), -np.sin(turn)]
    high = [mat.astype(BF16) for mat in mats]
    low = [(mat - h.astype(np.float64)).astype(BF16) for mat, h in zip(mats, high)]
    return np.stack(high + low)


def twiddle_table(ny):
    turn = np.arange(ny // 2) * (2.0 * np.pi / ny)
    rows = np.zeros((8, ny // 2), np.float32)
    rows[0], rows[1] = np.cos(turn), np.sin(turn)
    return rows


def split(value):
    high = value.astype(BF16)
    low = (value - high.astype(F32)).astype(BF16)
    return high, low


def cat(values, axis):
    return jnp.concatenate(values, axis=axis)


def block(a, b, c, d):
    return cat([cat([a, b], 1), cat([c, d], 1)], 0)


def dot_data_left(data, high, low):
    d_high, d_low = split(data)
    return jnp.dot(cat([d_high, d_low, d_high], 1), cat([high, high, low], 0), preferred_element_type=F32)


def dot_data_right(high, low, data):
    d_high, d_low = split(data)
    return jnp.dot(cat([high, high, low], 1), cat([d_high, d_low, d_high], 0), preferred_element_type=F32)


def sincos(x):
    turns = jnp.floor(x * (1.0 / math.pi) + 0.5)
    r = (x - turns * PI_HI) - turns * PI_LO
    sign = 1.0 - 2.0 * (turns - 2.0 * jnp.floor(turns * 0.5))
    r2 = r * r
    sin_p = 1.0 / math.factorial(11) * -1.0
    for k, sg in ((9, 1.0), (7, -1.0), (5, 1.0), (3, -1.0)):
        sin_p = sin_p * r2 + sg / math.factorial(k)
    sin_p = r + r * (r2 * sin_p)
    cos_p = 1.0 / math.factorial(12)
    for k, sg in ((10, -1.0), (8, 1.0), (6, -1.0), (4, 1.0), (2, -1.0), (0, 1.0)):
        cos_p = cos_p * r2 + sg / math.factorial(k)
    return sign * sin_p, sign * cos_p


def kernel(
    count, fields, freq, sidx, table, xs_in, ys_in, tw_in, image_out, fields_out,
    own, work, made, got, index, planes, levels, xs, ys, tw, wsq, omegas, means, turns,
    part_out, part_in, raw_out, raw_near, raw_far, first,
    in_sems, far_send, far_recv, tile_send, tile_recv, pair_send, pair_recv,
    near_send, near_recv, edge_send, edge_recv,
):
    me = lax.axis_index("slab")
    nx, ny = index.shape[1:]
    half = ny // 2
    unit = nx // sum(SHARES)
    starts = [unit * sum(SHARES[:j]) for j in range(CHUNKS)]

    def part_of(j):
        return pl.ds(starts[j], unit * SHARES[j])

    odd = lax.rem(me, 2) == 1
    even = jnp.logical_not(odd)
    down = me + 2 < count
    up = me >= 2
    straight = jnp.logical_and(up, lax.rem(me // 2, 2) == 0)

    def to(offset):
        return {"slab": jnp.clip(me + offset, 0, count - 1)}

    barrier = pltpu.get_barrier_semaphore()

    @pl.when(odd)
    def _():
        pl.semaphore_signal(barrier, inc=1, device_id=to(-1))

        @pl.when(down)
        def _():
            pl.semaphore_signal(barrier, inc=1, device_id=to(1))

    @pl.when(even)
    def _():
        pl.semaphore_signal(barrier, inc=1, device_id=to(1))

        @pl.when(up)
        def _():
            pl.semaphore_signal(barrier, inc=1, device_id=to(-1))

    @pl.when(down)
    def _():
        pl.semaphore_signal(barrier, inc=1, device_id=to(2))

    @pl.when(up)
    def _():
        pl.semaphore_signal(barrier, inc=1, device_id=to(-2))

    loads = [
        pltpu.make_async_copy(fields.at[0, 0], own.at[0], in_sems.at[0]),
        pltpu.make_async_copy(xs_in, xs, in_sems.at[1]),
        pltpu.make_async_copy(table, levels, in_sems.at[2]),
        pltpu.make_async_copy(sidx.at[0], index.at[0], in_sems.at[3]),
        pltpu.make_async_copy(ys_in, ys, in_sems.at[4]),
        pltpu.make_async_copy(tw_in, tw, in_sems.at[5]),
        pltpu.make_async_copy(fields.at[0, 1], own.at[1], in_sems.at[6]),
    ]
    for load in loads:
        load.start()

    row = lax.broadcasted_iota(jnp.int32, (nx, half), 0)
    wave_x = jnp.where(row < (nx + 1) // 2, row, row - nx).astype(F32) * (2.0 * math.pi / nx)
    lane = lax.broadcasted_iota(jnp.int32, (1, half), 1)
    for parity in (0, 1):
        k = 2 * lane + parity
        wave_y = jnp.where(k < (ny + 1) // 2, k, k - ny).astype(F32) * (2.0 * math.pi / ny)
        wsq[pl.ds(parity * nx, nx)] = wave_x * wave_x + wave_y * wave_y

    omegas[0] = jnp.full((8, 128), 1.0 + freq[0].astype(F32) / NFREQ, F32)

    @pl.when(jnp.logical_not(up))
    def _():
        got[...] = jnp.zeros(got.shape, F32)
        omegas[1] = jnp.zeros((8, 128), F32)

    @pl.when(jnp.logical_not(jnp.logical_or(odd & down, even & up)))
    def _():
        raw_far[...] = jnp.zeros((nx, ny), F32)

    def look_up(slot):
        pieces = [
            jnp.broadcast_to(levels[pl.ds(j * 128, 128)].reshape(1, 128), (nx, 128))
            for j in range(levels.shape[0] // 128)
        ]
        for h in range(ny // 128):
            cols = pl.ds(h * 128, 128)
            idx = index[slot, :, cols]
            inner = idx & 127
            value = jnp.take_along_axis(pieces[0], inner, axis=1, mode="promise_in_bounds")
            for j in range(1, len(pieces)):
                other = jnp.take_along_axis(pieces[j], inner, axis=1, mode="promise_in_bounds")
                value = jnp.where(idx >= j * 128, other, value)
            planes[slot, :, cols] = value
        columns = jnp.sum(planes[slot], axis=0, keepdims=True)
        return jnp.sum(columns, axis=1, keepdims=True) * (1.0 / (nx * ny))

    def phases(omega, mean_slow):
        q = (omega * mean_slow) ** 2 - wsq[...]
        root = jnp.sqrt(jnp.abs(q))
        sin_v, cos_v = sincos(root)
        moving = q > 0.0
        scale = 1.0 / (nx * ny)
        cos_p = jnp.where(moving, cos_v, jnp.exp(-root)) * scale
        sin_p = jnp.where(moving, sin_v, 0.0) * scale
        return cos_p, sin_p

    def screens(omega, slot, mean_slow):
        return sincos(omega * (planes[slot] - mean_slow))

    def spectral(source, which, phase):
        x_c, x_s, x_n = ((xs[i], xs[i + 3]) for i in range(3))
        y_c, y_s, y_n = ((ys[i], ys[i + 3]) for i in range(3))
        x_fwd = [block(x_c[i], x_s[i], x_n[i], x_c[i]) for i in (0, 1)]
        x_inv = [block(x_c[i], x_n[i], x_s[i], x_c[i]) for i in (0, 1)]
        y_fwd = [block(y_c[i], y_n[i], y_s[i], y_c[i]) for i in (0, 1)]
        y_inv = [block(y_c[i], y_s[i], y_n[i], y_c[i]) for i in (0, 1)]
        tw_c, tw_s = tw[:1], tw[1:2]
        cos_p, sin_p = phase
        mixed = []
        for f in which:
            spec = dot_data_right(*x_fwd, cat([source[f, 0], source[f, 1]], 0))
            left, right = spec[:, :half], spec[:, half:]
            plus, minus = left + right, left - right
            m_re, m_im = minus[:nx], minus[nx:]
            mixed.append(cat([
                cat([plus[:nx], plus[nx:]], 1),
                cat([m_re * tw_c + m_im * tw_s, m_im * tw_c - m_re * tw_s], 1),
            ], 0))
        spectrum = dot_data_left(cat(mixed, 0), *y_fwd)
        shifted = []
        for at, f in enumerate(which):
            v = spectrum[at * 2 * nx:(at + 1) * 2 * nx]
            v_re, v_im = v[:, :half], v[:, half:]
            if f == 0:
                shifted.append(cat([v_re * cos_p - v_im * sin_p, v_re * sin_p + v_im * cos_p], 1))
            else:
                shifted.append(cat([v_re * cos_p + v_im * sin_p, v_im * cos_p - v_re * sin_p], 1))
        back = dot_data_left(cat(shifted, 0), *y_inv)
        out = []
        for at, f in enumerate(which):
            b = back[at * 2 * nx:(at + 1) * 2 * nx]
            e_re, e_im = b[:nx, :half], b[:nx, half:]
            t_re, t_im = b[nx:, :half], b[nx:, half:]
            o_re, o_im = t_re * tw_c - t_im * tw_s, t_im * tw_c + t_re * tw_s
            moved = dot_data_right(*x_inv, cat([
                cat([e_re + o_re, e_re - o_re], 1), cat([e_im + o_im, e_im - o_im], 1),
            ], 0))
            out.append((moved[:nx], moved[nx:]))
        return out

    def turned(f, b_re, b_im, screen):
        s_sin, s_cos = screen
        if f == 0:
            return b_re * s_cos - b_im * s_sin, b_re * s_sin + b_im * s_cos
        return b_re * s_cos + b_im * s_sin, b_im * s_cos - b_re * s_sin

    def step(source, target, which, phase, screen):
        for f, (b_re, b_im) in zip(which, spectral(source, which, phase)):
            target[f, 0], target[f, 1] = turned(f, b_re, b_im, screen)

    def product(ref):
        return ref[0, 0] * ref[1, 0] + ref[0, 1] * ref[1, 1]

    def omega_of(slot):
        return omegas[slot, :1, :1]

    def remote(src, dst, send, recv, offset):
        return pltpu.make_async_remote_copy(
            src_ref=src, dst_ref=dst, send_sem=send, recv_sem=recv, device_id=to(offset)
        )

    def field_copy(f):
        return remote(made.at[f], got.at[f], far_send.at[f], far_recv.at[f], 2)

    def omega_copy():
        return remote(omegas.at[0], omegas.at[1], far_send.at[2], far_recv.at[2], 2)

    def mean_copy():
        return remote(means.at[0], means.at[1], far_send.at[3], far_recv.at[3], -2)

    def tile_copy(j):
        part = part_of(j)
        return remote(
            made.at[1, :, part], got.at[1, :, part], tile_send.at[j], tile_recv.at[j], 2
        )

    def index_copy(offset):
        return remote(sidx.at[0], index.at[1], pair_send.at[0], pair_recv.at[0], offset)

    def part_copy(offset):
        return remote(part_out, part_in, pair_send.at[1], pair_recv.at[1], offset)

    def near_copy(j, offset):
        part = part_of(j)
        return remote(raw_out.at[part], raw_near.at[part], near_send.at[j], near_recv.at[j], offset)

    def edge_copy(j, offset):
        part = part_of(j)
        return remote(raw_out.at[part], raw_far.at[part], edge_send.at[j], edge_recv.at[j], offset)

    def pass_copy(source, offset):
        return remote(source, raw_far, far_send.at[4], far_recv.at[4], offset)

    chunks = range(CHUNKS)

    @pl.when(odd)
    def _():
        for load in loads[:6]:
            load.wait()
        mean_own = look_up(0)
        phase = phases(omega_of(0), mean_own)
        screen_own = screens(omega_of(0), 0, mean_own)
        step(own, made, (0,), phase, screen_own)
        pl.semaphore_wait(barrier, 1 + jnp.where(down, 2, 0) + jnp.where(up, 1, 0))

        @pl.when(down)
        def _():
            omega_copy().start()
            field_copy(0).start()

        index_copy(-1).start()
        loads[6].wait()
        step(own, made, (1,), phase, screen_own)

        @pl.when(down)
        def _():
            field_copy(1).start()

        first[...] = product(made)
        index_copy(1).wait_recv()

        @pl.when(up)
        def _():
            omega_copy().wait_recv()

        mean_low = look_up(1)
        phase_0 = phases(omega_of(1), mean_low)
        screen_0 = screens(omega_of(1), 1, mean_low)
        phase_1 = phases(omega_of(1), mean_own)
        screen_1 = screens(omega_of(1), 0, mean_own)

        @pl.when(up)
        def _():
            field_copy(0).wait_recv()

        step(got, work, (0,), phase_0, screen_0)
        step(work, fields_out.at[0], (0,), phase_1, screen_1)

        @pl.when(up)
        def _():
            field_copy(1).wait_recv()

        step(got, work, (1,), phase_0, screen_0)
        part_out[...] = product(work)
        part_copy(-1).start()
        step(work, fields_out.at[0], (1,), phase_1, screen_1)
        part_copy(1).wait_recv()
        raw_out[...] = first[...] + part_in[...] + product(fields_out.at[0])
        @pl.when(jnp.logical_and(down, straight))
        def _():
            pass_copy(raw_out, 1).start()

        for j in chunks:
            near_copy(j, -1).start()

        for j in chunks:
            part = part_of(j)
            near_copy(j, 1).wait_recv()

            @pl.when(down)
            def _():
                edge_copy(j, -1).wait_recv()

            image_out[0, part] = raw_out[part] - 0.25 * (raw_near[part] + raw_far[part])

        index_copy(-1).wait_send()
        part_copy(-1).wait_send()
        for j in chunks:
            near_copy(j, -1).wait_send()

        @pl.when(down)
        def _():
            omega_copy().wait_send()
            field_copy(0).wait_send()
            field_copy(1).wait_send()

        @pl.when(jnp.logical_and(down, straight))
        def _():
            pass_copy(raw_out, 1).wait_send()

    @pl.when(even)
    def _():
        for load in loads:
            load.wait()
        mean_own = look_up(0)
        means[0] = jnp.broadcast_to(mean_own, (8, 128))
        pl.semaphore_wait(barrier, 1 + jnp.where(down, 1, 0) + jnp.where(up, 2, 0))

        @pl.when(up)
        def _():
            mean_copy().start()

        @pl.when(down)
        def _():
            omega_copy().start()

        index_copy(1).start()
        phase = phases(omega_of(0), mean_own)
        screen = screens(omega_of(0), 0, mean_own)
        step(own, work, (0, 1), phase, screen)
        first[...] = product(work)
        index_copy(-1).wait_recv()
        mean_next = look_up(1)
        phase = phases(omega_of(0), mean_next)
        screen = screens(omega_of(0), 1, mean_next)
        step(work, own, (0, 1), phase, screen)
        part_out[...] = product(own)
        part_copy(1).start()

        @pl.when(down)
        def _():
            mean_copy().wait_recv()
            phase = phases(omega_of(0), means[1, :1, :1])
            made[0, 0], made[0, 1] = spectral(own, (0,), phase)[0]
            field_copy(0).start()
            made[1, 0], made[1, 1] = spectral(own, (1,), phase)[0]
            for j in chunks:
                tile_copy(j).start()

        @pl.when(up)
        def _():
            omega_copy().wait_recv()

        turns[0], turns[1] = screens(omega_of(1), 0, means[0, :1, :1])
        part_copy(-1).wait_recv()
        first[...] = first[...] + part_in[...]

        @pl.when(up)
        def _():
            field_copy(0).wait_recv()

        for j in chunks:
            part = part_of(j)
            if j == 1:
                for i in chunks:
                    near_copy(i, -1).wait_recv()

                @pl.when(jnp.logical_and(down, jnp.logical_not(straight)))
                def _():
                    field_copy(0).wait_send()
                    tile_copy(0).wait_send()
                    pass_copy(raw_near, 2).start()

            @pl.when(up)
            def _():
                tile_copy(j).wait_recv()

            screen = turns[0, part], turns[1, part]
            s_re, s_im = turned(0, got[0, 0, part], got[0, 1, part], screen)
            r_re, r_im = turned(1, got[1, 0, part], got[1, 1, part], screen)
            raw_out[part] = first[part] + s_re * r_re + s_im * r_im

            @pl.when(up)
            def _():
                edge_copy(j, -1).start()

            if j == CHUNKS - 1:
                for i in chunks:
                    near_copy(i, 1).start()

            fields_out[0, 0, 0, part], fields_out[0, 0, 1, part] = s_re, s_im
            fields_out[0, 1, 0, part], fields_out[0, 1, 1, part] = r_re, r_im

        @pl.when(up)
        def _():
            pass_copy(raw_near, 2).wait_recv()

        image_out[0] = raw_out[...] - 0.25 * (raw_near[...] + raw_far[...])

        index_copy(1).wait_send()
        part_copy(1).wait_send()
        for j in chunks:
            near_copy(j, 1).wait_send()

        @pl.when(down)
        def _():
            omega_copy().wait_send()
            for j in range(1, CHUNKS):
                tile_copy(j).wait_send()

        @pl.when(jnp.logical_and(down, straight))
        def _():
            field_copy(0).wait_send()
            tile_copy(0).wait_send()

        @pl.when(jnp.logical_and(down, jnp.logical_not(straight)))
        def _():
            pass_copy(raw_near, 2).wait_send()

        @pl.when(up)
        def _():
            mean_copy().wait_send()
            for j in chunks:
                edge_copy(j, -1).wait_send()


def store(image, fields, image_out, fields_out, sems):
    copies = [
        pltpu.make_async_copy(fields, fields_out, sems.at[0]),
        pltpu.make_async_copy(image, image_out, sems.at[1]),
    ]
    for copy in copies:
        copy.start()
    for copy in copies:
        copy.wait()


def body(fields, freq_index, slowness_index, slowness_table):
    nx, ny = slowness_index.shape[1:]
    count = lax.axis_size("slab")
    assert slowness_index.shape[0] == 1 and count % 2 == 0
    half = ny // 2
    xs, ys, tw = dft_table(nx), dft_table(half), twiddle_table(ny)
    any_spec = pl.BlockSpec(memory_space=pl.ANY)
    vmem_spec = pl.BlockSpec(memory_space=pltpu.VMEM)
    plane = (nx, ny)
    dma = pltpu.SemaphoreType.DMA
    image, moved = pl.pallas_call(
        functools.partial(kernel, count),
        out_shape=(pltpu.VMEM((1, nx, ny), F32), pltpu.VMEM(fields.shape, F32)),
        in_specs=[
            any_spec, pl.BlockSpec(memory_space=pltpu.SMEM), any_spec, any_spec,
            any_spec, any_spec, any_spec,
        ],
        out_specs=(vmem_spec, vmem_spec),
        scratch_shapes=[
            pltpu.VMEM((2, 2) + plane, F32),
            pltpu.VMEM((2, 2) + plane, F32),
            pltpu.VMEM((2, 2) + plane, F32),
            pltpu.VMEM((2, 2) + plane, F32),
            pltpu.VMEM((2,) + plane, jnp.int32),
            pltpu.VMEM((2,) + plane, F32),
            pltpu.VMEM(slowness_table.shape, F32),
            pltpu.VMEM(xs.shape, BF16),
            pltpu.VMEM(ys.shape, BF16),
            pltpu.VMEM(tw.shape, F32),
            pltpu.VMEM((2 * nx, half), F32),
            pltpu.VMEM((2, 8, 128), F32),
            pltpu.VMEM((2, 8, 128), F32),
            pltpu.VMEM((2,) + plane, F32),
            pltpu.VMEM(plane, F32),
            pltpu.VMEM(plane, F32),
            pltpu.VMEM(plane, F32),
            pltpu.VMEM(plane, F32),
            pltpu.VMEM(plane, F32),
            pltpu.VMEM(plane, F32),
            dma((7,)),
            dma((5,)),
            dma((5,)),
            dma((CHUNKS,)),
            dma((CHUNKS,)),
            dma((2,)),
            dma((2,)),
            dma((CHUNKS,)),
            dma((CHUNKS,)),
            dma((CHUNKS,)),
            dma((CHUNKS,)),
        ],
        compiler_params=pltpu.CompilerParams(collective_id=0, has_side_effects=True),
        name="slabs",
    )(
        fields, freq_index, slowness_index, slowness_table,
        jnp.asarray(xs), jnp.asarray(ys), jnp.asarray(tw),
    )
    return pl.pallas_call(
        store,
        out_shape=(
            jax.ShapeDtypeStruct((1, nx, ny), F32),
            jax.ShapeDtypeStruct(fields.shape, F32),
        ),
        in_specs=[vmem_spec, vmem_spec],
        out_specs=(any_spec, any_spec),
        scratch_shapes=[dma((2,))],
        name="store",
    )(
        pltpu.with_memory_space_constraint(image, pltpu.VMEM),
        pltpu.with_memory_space_constraint(moved, pltpu.VMEM),
    )


def solution(mesh):
    return jax.shard_map(
        body,
        mesh=mesh,
        in_specs=(
            P(("shots", "slab"), None, None, None, None),
            P(("shots", "slab")),
            P("slab", None, None),
            P(),
        ),
        out_specs=(P(("shots", "slab"), None, None), P(("shots", "slab"), None, None, None, None)),
        check_vma=False,
    )
```
